256 devices in a mesh: row: 16 (over y, x), col: 16 (over z, core).
Axes of the slice: x: 4, y: 4, z: 8, core: 2. Of those that a mesh axis runs over, the one named last changes fastest.
Arguments:
- matrix: float32 [2, 4096, 2, 4096], P(None, 'row', None, 'col'), may hold values from -8 to 8, as said below
Outputs:
- reduced: float32 [2, 4096, 2, 4096], P(None, 'row', None, 'col')
The draws below stay inside these ranges and needn't reach their ends.
Inputs may be any that keep to these rules, and one draw needn't show every extreme that they name: symmetric: the entries at (r, c) and (c, r) of the 8192 x 8192 matrix are equal.
All inputs are finite; a program needn't handle non-finite values.
Results may differ from the reference program's by a relative error of at most 0.0002.
Values sent between devices are 32-bit elements; how exact they have to be, the bound alone decides.
No kernel may reach another device: no remote copies, remote signals or barrier semaphores. Data moves between devices by JAX's collectives and lax.ppermute only.
A program may use at most 64 MiB of HBM per device.

```python
import jax
import jax.numpy as jnp
from jax import lax

N = 8192
NB = 256
PANELS = 2
KR = 2
KC = 2
N_ROW = 16
N_COL = 16


def draw_matrix(key, part):
    base = jax.random.normal(jax.random.fold_in(key, 11), (N, N), jnp.float32)
    sym = (base + base.T) * 0.5
    sym = jnp.clip(sym, -8.0, 8.0)
    heavy = jax.random.uniform(jax.random.fold_in(key, 13), (NB, NB), jnp.float32, -8.0, 8.0)
    sym = sym.at[NB:2 * NB, 0:NB].set(heavy)
    sym = sym.at[0:NB, NB:2 * NB].set(heavy.T)
    return sym.reshape(KR, N_ROW * NB, KC, N_COL * NB)


def setup_inputs(seed: int = 0) -> dict:
    keys = jax.random.split(jax.random.key(seed), 2)
    return {
        "matrix": draw_matrix(jax.random.fold_in(keys[1], 71), 0),
    }


highest = lax.Precision.HIGHEST

def matmul(left, right):
    return jnp.dot(left.astype(jnp.float32), right.astype(jnp.float32), precision=highest, preferred_element_type=jnp.float32)

def reference(matrix):
    order = matrix.shape[0] * matrix.shape[1]
    dense = matrix.reshape(order, order)
    for panel in range(PANELS):
        first = panel * NB
        start = first + NB
        strip = dense[start:, first:start]
        factor = jnp.linalg.cholesky(matmul(strip.T, strip))
        basis = jax.scipy.linalg.solve_triangular(factor, strip.T, lower=True).T
        shifted = jnp.eye(NB, dtype=jnp.float32) + basis[:NB]
        normal = matmul(shifted.T, shifted)
        coupling = jax.scipy.linalg.cho_solve((jnp.linalg.cholesky(normal), True), shifted.T)
        vectors = basis.at[:NB].add(jnp.eye(NB, dtype=jnp.float32))
        trailing = dense[start:, start:]
        applied = matmul(trailing, vectors)
        middle = matmul(matmul(coupling, matmul(vectors.T, applied)), coupling.T)
        factor_y = matmul(applied, coupling.T) - 0.5 * matmul(vectors, middle)
        trailing = trailing - matmul(factor_y, vectors.T) - matmul(vectors, factor_y.T)
        block = jnp.zeros_like(strip).at[:NB].set(-factor.T)
        dense = dense.at[start:, start:].set(trailing)
        dense = dense.at[start:, first:start].set(block)
        dense = dense.at[first:start, start:].set(block.T)
    return dense.reshape(matrix.shape)
```

```python
import functools

import jax
import jax.numpy as jnp
from jax import lax
from jax.experimental import pallas as pl
from jax.experimental.pallas import tpu as pltpu
from jax.sharding import Mesh
from jax.sharding import PartitionSpec as P

PANELS = 2
COL = ("col_0", "col_1")

highest = lax.Precision.HIGHEST
high = lax.Precision.HIGH


def product(left, right, dims=((1,), (0,)), precision=high):
    return lax.dot_general(
        left, right, (dims, ((), ())), precision=precision, preferred_element_type=jnp.float32
    )


NT = ((1,), (1,))
TN = ((0,), (0,))
GROUP = 8


def row_of(tile, s):
    return jnp.broadcast_to(tile[s : s + 1, :], (8, 128))


class Elimination:
    def __init__(self, window, off, b):
        self.b, self.off, self.count = b, off, b // 8
        self.sublane = lax.broadcasted_iota(jnp.int32, (8, 128), 0)
        lanes = lax.broadcasted_iota(jnp.int32, (8, 128), 1)
        self.a = [window[8 * i : 8 * i + 8, :] for i in range(self.count)]
        self.e = [(lanes == self.sublane + 8 * i).astype(jnp.float32) for i in range(self.count)]
        zero = jnp.zeros((8, 128), jnp.float32)
        self.low = [zero] * self.count
        self.inv = [zero] * self.count

    def group(self, t):
        tiles = range(self.count)
        first = self.off + GROUP * t
        cols = [
            [jnp.broadcast_to(self.a[i][:, first + q : first + q + 1], (8, 128)) for i in tiles]
            for q in range(GROUP)
        ]
        for q in range(GROUP):
            inv = 1.0 / row_of(cols[q][t], q)
            here = self.sublane == q
            scale = [cols[q][i] * inv for i in tiles]
            scale[t] = jnp.where(here, 0.0, scale[t])
            for p in range(q + 1, GROUP):
                head = row_of(cols[p][t], q)
                for i in tiles:
                    cols[p][i] = cols[p][i] - scale[i] * head
            self.inv[t] = jnp.where(here, inv, self.inv[t])
            self.low[t] = jnp.where(here, self.e[t], self.low[t])
            row_a = row_of(self.a[t], q)
            row_e = row_of(self.e[t], q)
            for i in tiles:
                self.a[i] = self.a[i] - scale[i] * row_a
                self.e[i] = self.e[i] - scale[i] * row_e

    def inverse(self):
        inv = jnp.concatenate(self.inv, axis=0)
        return (jnp.concatenate(self.e, axis=0) * inv)[:, : self.b]

    def lower_inverse(self):
        inv = jnp.concatenate(self.inv, axis=0)
        return (jnp.concatenate(self.low, axis=0) * jnp.sqrt(inv))[:, : self.b]


def factor_kernel(g_ref, x_ref, r_ref, t_ref, aa, xb, wb, *, b):
    exact = functools.partial(product, precision=highest)
    n = g_ref.shape[0]
    count = n // b
    rows = lax.broadcasted_iota(jnp.int32, (n, n), 0)
    cols = lax.broadcasted_iota(jnp.int32, (n, n), 1)
    aa[:, :n] = g_ref[...]
    aa[:, n:] = (rows == cols).astype(jnp.float32)
    xb[:, :n] = x_ref[...]
    xb[:, n:] = jnp.zeros((n, n), jnp.float32)
    wb[...] = jnp.zeros((128, 2 * n), jnp.float32)
    lane = lax.broadcasted_iota(jnp.int32, (n, 128), 1)
    row = lax.broadcasted_iota(jnp.int32, (n, 128), 0)
    second = None
    for k in range(count + 1):
        lo, hi = k * b, (k + 1) * b
        win, off = lo // 128 * 128, lo % 128
        running = []
        if k < count:
            first = Elimination(aa[lo:hi, win : win + 128], off, b)
            running.append(first)
        if k > 0:
            second = Elimination(pivot, (lo - b) % 128, b)
            running.append(second)
        for t in range(b // 8):
            for one in running:
                one.group(t)
        if k < count:
            block = aa[lo:hi, :]
            if hi < n:
                wb[off : off + b, :] = exact(first.inverse(), block)
                keep = (lane[: n - hi] >= off) & (lane[: n - hi] < off + b)
                left = jnp.where(keep, aa[hi:, win : win + 128], 0.0)
                aa[hi:, :] = aa[hi:, :] - exact(left, wb[...])
            upper = exact(first.lower_inverse(), block)
            wide_row = lax.broadcasted_iota(jnp.int32, (b, 2 * n), 0) + lo
            wide_col = lax.broadcasted_iota(jnp.int32, (b, 2 * n), 1)
            upper = jnp.where(wide_col >= wide_row, upper, 0.0)
            upper = jnp.where(wide_col - n > wide_row, 0.0, upper)
            r_ref[lo:hi, :] = upper[:, :n]
        if k > 0:
            plo, phi = lo - b, lo
            pwin, poff = plo // 128 * 128, plo % 128
            xb[plo:phi, :] = exact(second.inverse(), pivot_row)
            keep = (lane >= poff) & (lane < poff + b) & ((row < plo) | (row >= phi))
            left = jnp.where(keep, xb[:, pwin : pwin + 128], 0.0)
            xb[...] = xb[...] - exact(left, xb[pwin : pwin + 128, :])
        if k < count:
            pivot_row = xb[lo:hi, :] + upper
            pivot = pivot_row[:, win : win + 128]
    t_ref[...] = xb[:, n:]


def factor(gram, top):
    n = gram.shape[0]
    square = jax.ShapeDtypeStruct((n, n), jnp.float32)
    return pl.pallas_call(
        functools.partial(factor_kernel, b=32),
        out_shape=(square, square),
        scratch_shapes=[
            pltpu.VMEM((n, 2 * n), jnp.float32),
            pltpu.VMEM((n, 2 * n), jnp.float32),
            pltpu.VMEM((128, 2 * n), jnp.float32),
        ],
        name="factor",
    )(gram, top)


def exchange(value, axis):
    return lax.all_to_all(value, axis, 0, 0, tiled=True)


def copied(value, axis):
    copies = jnp.broadcast_to(value, (lax.axis_size(axis), *value.shape))
    return exchange(copies, axis)


def transposed(value):
    rows = lax.axis_size("row")
    cols = lax.axis_size(COL)
    pairs = [(r * cols + c, c * rows + r) for r in range(rows) for c in range(cols)]
    return lax.ppermute(value, ("row", *COL), pairs)


def shards(matrix):
    row_blocks, width, col_blocks, _ = matrix.shape
    devices = lax.axis_size("row")
    row_index = lax.axis_index("row")
    col_index = lax.axis_index(COL)
    local = row_blocks * width
    part = width // devices
    dense = matrix.reshape(local, local)
    offsets = jnp.arange(local, dtype=jnp.int32)
    global_rows = (offsets // width * devices + row_index) * width + offsets % width
    global_cols = (offsets // width * devices + col_index) * width + offsets % width
    corners = []
    for panel in range(PANELS):
        start = (panel + 1) * width
        below_cols = global_cols[None, :] >= start
        below_rows = global_rows[None, :] >= start
        sent = exchange(dense[:width].reshape(devices, part, local), "row")
        mine = jnp.where(below_cols, sent[panel : panel + 2].reshape(2 * part, local), 0.0)
        both = copied(mine, "row")
        x_cols = both[:, :part].reshape(width, local)
        c_cols = both[:, part:].reshape(width, local)
        x_rows = transposed(x_cols)
        c_rows = transposed(c_cols)
        own = row_index * part
        gram_part = product(
            lax.dynamic_slice_in_dim(x_cols, own, part, 0), x_cols, NT, highest
        )
        top_part = jnp.where(col_index == panel + 1, mine[:part, :width], 0.0)
        sums = jnp.sum(copied(jnp.concatenate([gram_part, top_part]), COL), axis=0)
        u_part = product(x_rows, dense)
        merged = jnp.concatenate(
            [
                jnp.broadcast_to(sums, (devices, 2 * part, width)),
                u_part.reshape(devices, 2 * part, width),
            ],
            axis=1,
        )
        merged = exchange(merged, "row")
        gram = merged[:, :part].reshape(width, width)
        top = merged[:, part : 2 * part].reshape(width, width).T
        u_own = jnp.sum(merged[:, 2 * part :], axis=0).reshape(part, local)
        u_cols = copied(u_own, "row").reshape(width, local)
        u_cols = jnp.where(below_cols, u_cols, 0.0)
        u_rows = transposed(u_cols)
        upper, core = factor(gram, top)
        lower = upper.T

        def with_top(x, index):
            head = jnp.where(index == panel + 1, lower, 0.0)
            return jnp.concatenate([x[:, :width] + head, x[:, width:]], axis=1)

        v_cols = with_top(x_cols, col_index)
        v_rows = with_top(x_rows, row_index)
        w_cols = u_cols + product(lower, c_cols)
        w_rows = u_rows + product(lower, c_rows)
        inner_part = product(lax.dynamic_slice_in_dim(v_cols, own, part, 0), w_cols, NT)
        inner_own = jnp.sum(copied(inner_part, COL), axis=0)
        inner = copied(inner_own, "row").reshape(width, width)
        middle = 0.5 * product(product(core, inner), core, NT)
        y_cols = product(core, w_cols) - product(middle, v_cols)
        y_rows = product(core, w_rows) - product(middle, v_rows)
        dense = dense - product(
            jnp.concatenate([y_rows, v_rows]), jnp.concatenate([v_cols, y_cols]), TN
        )
        corners.append(upper)
    slot_rows = offsets[:, None] < width
    slot_cols = offsets[None, :] < width
    for panel, upper in enumerate(corners):
        start = (panel + 1) * width
        pad = ((0, local - width), (0, local - width))
        at_cols = (col_index == panel) & slot_cols & (global_rows[:, None] >= start)
        new_cols = jnp.where(row_index == panel + 1, -jnp.pad(upper, pad), 0.0)
        dense = jnp.where(at_cols, new_cols, dense)
        at_rows = (row_index == panel) & slot_rows & (global_cols[None, :] >= start)
        new_rows = jnp.where(col_index == panel + 1, -jnp.pad(upper.T, pad), 0.0)
        dense = jnp.where(at_rows, new_rows, dense)
    return dense.reshape(matrix.shape)


def solution(mesh):
    split = Mesh(mesh.devices.reshape(mesh.shape["row"], 8, 2), ("row", "col_0", "col_1"))
    placed = (P(None, "row", None, COL),)
    return jax.shard_map(
        shards, mesh=split, in_specs=placed, out_specs=P(None, "row", None, COL), check_vma=False
    )
```

```python
import functools

import jax
import jax.numpy as jnp
from jax import lax
from jax.experimental import pallas as pl
from jax.experimental.pallas import tpu as pltpu
from jax.sharding import Mesh
from jax.sharding import PartitionSpec as P

PANELS = 2
COL = ("col_0", "col_1")

highest = lax.Precision.HIGHEST
high = lax.Precision.HIGH


def product(left, right, dims=((1,), (0,)), precision=high):
    return lax.dot_general(
        left, right, (dims, ((), ())), precision=precision, preferred_element_type=jnp.float32
    )


NT = ((1,), (1,))
TN = ((0,), (0,))
GROUP = 8


def row_of(tile, s):
    return jnp.broadcast_to(tile[s : s + 1, :], (8, 128))


class Elimination:
    def __init__(self, window, off, b):
        self.b, self.off, self.count = b, off, b // 8
        self.sublane = lax.broadcasted_iota(jnp.int32, (8, 128), 0)
        lanes = lax.broadcasted_iota(jnp.int32, (8, 128), 1)
        self.a = [window[8 * i : 8 * i + 8, :] for i in range(self.count)]
        self.e = [(lanes == self.sublane + 8 * i).astype(jnp.float32) for i in range(self.count)]
        zero = jnp.zeros((8, 128), jnp.float32)
        self.low = [zero] * self.count
        self.inv = [zero] * self.count

    def group(self, t):
        tiles = range(self.count)
        first = self.off + GROUP * t
        cols = [
            [jnp.broadcast_to(self.a[i][:, first + q : first + q + 1], (8, 128)) for i in tiles]
            for q in range(GROUP)
        ]
        for q in range(GROUP):
            inv = 1.0 / row_of(cols[q][t], q)
            here = self.sublane == q
            scale = [cols[q][i] * inv for i in tiles]
            scale[t] = jnp.where(here, 0.0, scale[t])
            for p in range(q + 1, GROUP):
                head = row_of(cols[p][t], q)
                for i in tiles:
                    cols[p][i] = cols[p][i] - scale[i] * head
            self.inv[t] = jnp.where(here, inv, self.inv[t])
            self.low[t] = jnp.where(here, self.e[t], self.low[t])
            row_a = row_of(self.a[t], q)
            row_e = row_of(self.e[t], q)
            for i in tiles:
                self.a[i] = self.a[i] - scale[i] * row_a
                self.e[i] = self.e[i] - scale[i] * row_e

    def inverse(self):
        inv = jnp.concatenate(self.inv, axis=0)
        return (jnp.concatenate(self.e, axis=0) * inv)[:, : self.b]

    def lower_inverse(self):
        inv = jnp.concatenate(self.inv, axis=0)
        return (jnp.concatenate(self.low, axis=0) * jnp.sqrt(inv))[:, : self.b]


def factor_kernel(g_ref, x_ref, r_ref, t_ref, aa, xb, wb, *, b):
    exact = functools.partial(product, precision=highest)
    n = g_ref.shape[0]
    count = n // b
    rows = lax.broadcasted_iota(jnp.int32, (n, n), 0)
    cols = lax.broadcasted_iota(jnp.int32, (n, n), 1)
    aa[:, :n] = g_ref[...]
    aa[:, n:] = (rows == cols).astype(jnp.float32)
    xb[:, :n] = x_ref[...]
    xb[:, n:] = jnp.zeros((n, n), jnp.float32)
    wb[...] = jnp.zeros((128, 2 * n), jnp.float32)
    lane = lax.broadcasted_iota(jnp.int32, (n, 128), 1)
    row = lax.broadcasted_iota(jnp.int32, (n, 128), 0)
    second = None
    for k in range(count + 1):
        lo, hi = k * b, (k + 1) * b
        win, off = lo // 128 * 128, lo % 128
        running = []
        if k < count:
            first = Elimination(aa[lo:hi, win : win + 128], off, b)
            running.append(first)
        if k > 0:
            second = Elimination(pivot, (lo - b) % 128, b)
            running.append(second)
        for t in range(b // 8):
            for one in running:
                one.group(t)
        if k < count:
            block = aa[lo:hi, :]
            if hi < n:
                wb[off : off + b, :] = exact(first.inverse(), block)
                keep = (lane[: n - hi] >= off) & (lane[: n - hi] < off + b)
                left = jnp.where(keep, aa[hi:, win : win + 128], 0.0)
                aa[hi:, :] = aa[hi:, :] - exact(left, wb[...])
            upper = exact(first.lower_inverse(), block)
            wide_row = lax.broadcasted_iota(jnp.int32, (b, 2 * n), 0) + lo
            wide_col = lax.broadcasted_iota(jnp.int32, (b, 2 * n), 1)
            upper = jnp.where(wide_col >= wide_row, upper, 0.0)
            upper = jnp.where(wide_col - n > wide_row, 0.0, upper)
            r_ref[lo:hi, :] = upper[:, :n]
        if k > 0:
            plo, phi = lo - b, lo
            pwin, poff = plo // 128 * 128, plo % 128
            xb[plo:phi, :] = exact(second.inverse(), pivot_row)
            keep = (lane >= poff) & (lane < poff + b) & ((row < plo) | (row >= phi))
            left = jnp.where(keep, xb[:, pwin : pwin + 128], 0.0)
            xb[...] = xb[...] - exact(left, xb[pwin : pwin + 128, :])
        if k < count:
            pivot_row = xb[lo:hi, :] + upper
            pivot = pivot_row[:, win : win + 128]
    t_ref[...] = xb[:, n:]


def factor(gram, top):
    n = gram.shape[0]
    square = jax.ShapeDtypeStruct((n, n), jnp.float32)
    return pl.pallas_call(
        functools.partial(factor_kernel, b=32),
        out_shape=(square, square),
        scratch_shapes=[
            pltpu.VMEM((n, 2 * n), jnp.float32),
            pltpu.VMEM((n, 2 * n), jnp.float32),
            pltpu.VMEM((128, 2 * n), jnp.float32),
        ],
        name="factor",
    )(gram, top)


def exchange(value, axis):
    return lax.all_to_all(value, axis, 0, 0, tiled=True)


def copied(value, axis):
    copies = jnp.broadcast_to(value, (lax.axis_size(axis), *value.shape))
    return exchange(copies, axis)


def transposed(value):
    rows = lax.axis_size("row")
    cols = lax.axis_size(COL)
    pairs = [(r * cols + c, c * rows + r) for r in range(rows) for c in range(cols)]
    return lax.ppermute(value, ("row", *COL), pairs)


def swapped(value):
    return lax.ppermute(value, COL[1], [(0, 1), (1, 0)])


def core_sum(value):
    return value + swapped(value)


def both_cores(lines):
    other = swapped(lines)
    second = lax.axis_index(COL[1]) == 1
    pair = [jnp.where(second, other, lines), jnp.where(second, lines, other)]
    return jnp.stack(pair, axis=1)


def join(parts):
    parts = parts.reshape(-1, *parts.shape[-3:])
    first, last = parts[:, 0], parts[:, 1]
    local = parts.shape[-1]
    return first.reshape(-1, local), last.reshape(-1, local)


def shards(matrix):
    row_blocks, width, col_blocks, _ = matrix.shape
    devices = lax.axis_size("row")
    row_index = lax.axis_index("row")
    col_index = lax.axis_index(COL)
    local = row_blocks * width
    part = width // devices
    dense = matrix.reshape(local, local)
    offsets = jnp.arange(local, dtype=jnp.int32)
    global_rows = (offsets // width * devices + row_index) * width + offsets % width
    global_cols = (offsets // width * devices + col_index) * width + offsets % width
    corners = []
    for panel in range(PANELS):
        start = (panel + 1) * width
        below_cols = global_cols[None, :] >= start
        below_rows = global_rows[None, :] >= start
        sent = exchange(dense[:width].reshape(devices, part, local), "row")
        sent = lax.slice_in_dim(sent, panel, panel + 2, axis=0)
        mine = jnp.where(below_cols, sent, 0.0)
        turned = transposed(mine[0])
        x_cols = copied(mine[0], "row").reshape(width, local)
        own = row_index * part
        gram_part = product(
            lax.dynamic_slice_in_dim(x_cols, own, part, 0), x_cols, NT, highest
        )
        top_part = jnp.where(col_index == panel + 1, mine[0, :, :width], 0.0)
        summed = core_sum(jnp.concatenate([gram_part, top_part]))
        lines = jnp.concatenate([summed.reshape(part, local), turned])
        lines = copied(lines, COL[0])
        sums = jnp.sum(lines[:, :part], axis=0).reshape(2 * part, width)
        x_rows = both_cores(lines[:, part:]).reshape(width, local)
        u_part = product(x_rows, dense)
        merged = jnp.concatenate(
            [
                jnp.broadcast_to(sums, (devices, 2 * part, width)),
                u_part.reshape(devices, 2 * part, width),
            ],
            axis=1,
        )
        merged = exchange(merged, "row")
        gram = merged[:, :part].reshape(width, width)
        top = merged[:, part : 2 * part].reshape(width, width).T
        u_own = jnp.sum(merged[:, 2 * part :], axis=0).reshape(part, local)
        pair = jnp.stack([jnp.where(below_cols, u_own, 0.0), mine[1]])
        u_cols, c_cols = join(copied(pair, "row"))
        u_rows, c_rows = join(both_cores(copied(transposed(pair), COL[0])))
        upper, core = factor(gram, top)
        lower = upper.T

        def with_top(x, index):
            head = jnp.where(index == panel + 1, lower, 0.0)
            return jnp.concatenate([x[:, :width] + head, x[:, width:]], axis=1)

        v_cols = with_top(x_cols, col_index)
        v_rows = with_top(x_rows, row_index)
        w_cols = u_cols + product(lower, c_cols)
        w_rows = u_rows + product(lower, c_rows)
        inner_part = product(lax.dynamic_slice_in_dim(v_cols, own, part, 0), w_cols, NT)
        inner_own = jnp.sum(copied(core_sum(inner_part), COL[0]), axis=0)
        inner = copied(inner_own, "row").reshape(width, width)
        middle = 0.5 * product(product(core, inner), core, NT)
        y_cols = product(core, w_cols) - product(middle, v_cols)
        y_rows = product(core, w_rows) - product(middle, v_rows)
        dense = dense - product(
            jnp.concatenate([y_rows, v_rows]), jnp.concatenate([v_cols, y_cols]), TN
        )
        corners.append(upper)
    slot_rows = offsets[:, None] < width
    slot_cols = offsets[None, :] < width
    for panel, upper in enumerate(corners):
        start = (panel + 1) * width
        pad = ((0, local - width), (0, local - width))
        at_cols = (col_index == panel) & slot_cols & (global_rows[:, None] >= start)
        new_cols = jnp.where(row_index == panel + 1, -jnp.pad(upper, pad), 0.0)
        dense = jnp.where(at_cols, new_cols, dense)
        at_rows = (row_index == panel) & slot_rows & (global_cols[None, :] >= start)
        new_rows = jnp.where(col_index == panel + 1, -jnp.pad(upper.T, pad), 0.0)
        dense = jnp.where(at_rows, new_rows, dense)
    return dense.reshape(matrix.shape)


def solution(mesh):
    split = Mesh(mesh.devices.reshape(mesh.shape["row"], 8, 2), ("row", "col_0", "col_1"))
    placed = (P(None, "row", None, COL),)
    return jax.shard_map(
        shards, mesh=split, in_specs=placed, out_specs=P(None, "row", None, COL), check_vma=False
    )
```

```python
import functools

import jax
import jax.numpy as jnp
from jax import lax
from jax.experimental import pallas as pl
from jax.experimental.pallas import tpu as pltpu
from jax.sharding import Mesh
from jax.sharding import PartitionSpec as P

PANELS = 2
COL = ("col_0", "col_1")

highest = lax.Precision.HIGHEST
high = lax.Precision.HIGH


def product(left, right, dims=((1,), (0,)), precision=high):
    return lax.dot_general(
        left, right, (dims, ((), ())), precision=precision, preferred_element_type=jnp.float32
    )


NT = ((1,), (1,))
TN = ((0,), (0,))
GROUP = 8


def row_of(tile, s):
    return jnp.broadcast_to(tile[s : s + 1, :], (8, 128))


class Elimination:
    def __init__(self, window, off, b):
        self.b, self.off, self.count = b, off, b // 8
        self.sublane = lax.broadcasted_iota(jnp.int32, (8, 128), 0)
        lanes = lax.broadcasted_iota(jnp.int32, (8, 128), 1)
        self.a = [window[8 * i : 8 * i + 8, :] for i in range(self.count)]
        self.e = [(lanes == self.sublane + 8 * i).astype(jnp.float32) for i in range(self.count)]
        zero = jnp.zeros((8, 128), jnp.float32)
        self.low = [zero] * self.count
        self.inv = [zero] * self.count

    def group(self, t):
        tiles = range(self.count)
        first = self.off + GROUP * t
        cols = [
            [jnp.broadcast_to(self.a[i][:, first + q : first + q + 1], (8, 128)) for i in tiles]
            for q in range(GROUP)
        ]
        for q in range(GROUP):
            inv = 1.0 / row_of(cols[q][t], q)
            here = self.sublane == q
            scale = [cols[q][i] * inv for i in tiles]
            scale[t] = jnp.where(here, 0.0, scale[t])
            for p in range(q + 1, GROUP):
                head = row_of(cols[p][t], q)
                for i in tiles:
                    cols[p][i] = cols[p][i] - scale[i] * head
            self.inv[t] = jnp.where(here, inv, self.inv[t])
            self.low[t] = jnp.where(here, self.e[t], self.low[t])
            row_a = row_of(self.a[t], q)
            row_e = row_of(self.e[t], q)
            for i in tiles:
                self.a[i] = self.a[i] - scale[i] * row_a
                self.e[i] = self.e[i] - scale[i] * row_e

    def inverse(self):
        inv = jnp.concatenate(self.inv, axis=0)
        return (jnp.concatenate(self.e, axis=0) * inv)[:, : self.b]

    def lower_inverse(self):
        inv = jnp.concatenate(self.inv, axis=0)
        return (jnp.concatenate(self.low, axis=0) * jnp.sqrt(inv))[:, : self.b]


def factor_kernel(g_ref, x_ref, r_ref, t_ref, aa, xb, wb, *, b):
    exact = functools.partial(product, precision=highest)
    n = g_ref.shape[0]
    count = n // b
    rows = lax.broadcasted_iota(jnp.int32, (n, n), 0)
    cols = lax.broadcasted_iota(jnp.int32, (n, n), 1)
    aa[:, :n] = g_ref[...]
    aa[:, n:] = (rows == cols).astype(jnp.float32)
    xb[:, :n] = x_ref[...]
    xb[:, n:] = jnp.zeros((n, n), jnp.float32)
    wb[...] = jnp.zeros((128, 2 * n), jnp.float32)
    lane = lax.broadcasted_iota(jnp.int32, (n, 128), 1)
    row = lax.broadcasted_iota(jnp.int32, (n, 128), 0)
    second = None
    for k in range(count + 1):
        lo, hi = k * b, (k + 1) * b
        win, off = lo // 128 * 128, lo % 128
        running = []
        if k < count:
            first = Elimination(aa[lo:hi, win : win + 128], off, b)
            running.append(first)
        if k > 0:
            second = Elimination(pivot, (lo - b) % 128, b)
            running.append(second)
        for t in range(b // 8):
            for one in running:
                one.group(t)
        if k < count:
            block = aa[lo:hi, :]
            if hi < n:
                wb[off : off + b, :] = exact(first.inverse(), block)
                keep = (lane[: n - hi] >= off) & (lane[: n - hi] < off + b)
                left = jnp.where(keep, aa[hi:, win : win + 128], 0.0)
                aa[hi:, :] = aa[hi:, :] - exact(left, wb[...])
            upper = exact(first.lower_inverse(), block)
            wide_row = lax.broadcasted_iota(jnp.int32, (b, 2 * n), 0) + lo
            wide_col = lax.broadcasted_iota(jnp.int32, (b, 2 * n), 1)
            upper = jnp.where(wide_col >= wide_row, upper, 0.0)
            upper = jnp.where(wide_col - n > wide_row, 0.0, upper)
            r_ref[lo:hi, :] = upper[:, :n]
        if k > 0:
            plo, phi = lo - b, lo
            pwin, poff = plo // 128 * 128, plo % 128
            xb[plo:phi, :] = exact(second.inverse(), pivot_row)
            keep = (lane >= poff) & (lane < poff + b) & ((row < plo) | (row >= phi))
            left = jnp.where(keep, xb[:, pwin : pwin + 128], 0.0)
            xb[...] = xb[...] - exact(left, xb[pwin : pwin + 128, :])
        if k < count:
            pivot_row = xb[lo:hi, :] + upper
            pivot = pivot_row[:, win : win + 128]
    t_ref[...] = xb[:, n:]


def factor(gram, top):
    n = gram.shape[0]
    square = jax.ShapeDtypeStruct((n, n), jnp.float32)
    return pl.pallas_call(
        functools.partial(factor_kernel, b=32),
        out_shape=(square, square),
        scratch_shapes=[
            pltpu.VMEM((n, 2 * n), jnp.float32),
            pltpu.VMEM((n, 2 * n), jnp.float32),
            pltpu.VMEM((128, 2 * n), jnp.float32),
        ],
        name="factor",
    )(gram, top)


def exchange(value, axis):
    return lax.all_to_all(value, axis, 0, 0, tiled=True)


def copied(value, axis):
    copies = jnp.broadcast_to(value, (lax.axis_size(axis), *value.shape))
    return exchange(copies, axis)


def transposed(value):
    rows = lax.axis_size("row")
    cols = lax.axis_size(COL)
    pairs = [(r * cols + c, c * rows + r) for r in range(rows) for c in range(cols)]
    return lax.ppermute(value, ("row", *COL), pairs)


def swapped(value):
    return lax.ppermute(value, COL[1], [(0, 1), (1, 0)])


def core_sum(value):
    return value + swapped(value)


def both_cores(lines):
    other = swapped(lines)
    second = lax.axis_index(COL[1]) == 1
    pair = [jnp.where(second, other, lines), jnp.where(second, lines, other)]
    return jnp.stack(pair, axis=1)


def join(parts):
    parts = parts.reshape(-1, *parts.shape[-3:])
    first, last = parts[:, 0], parts[:, 1]
    local = parts.shape[-1]
    return first.reshape(-1, local), last.reshape(-1, local)


def shards(matrix):
    row_blocks, width, _, _ = matrix.shape
    devices = lax.axis_size("row")
    row_index = lax.axis_index("row")
    col_index = lax.axis_index(COL)
    local = row_blocks * width
    part = width // devices
    dense = matrix.reshape(local, local)
    offsets = jnp.arange(local, dtype=jnp.int32)
    global_rows = (offsets // width * devices + row_index) * width + offsets % width
    global_cols = (offsets // width * devices + col_index) * width + offsets % width
    own = row_index * part
    corners = []
    sent = exchange(dense[:width].reshape(devices, part, local), "row")
    for panel in range(PANELS):
        start = (panel + 1) * width
        last = panel + 1 == PANELS
        below_cols = global_cols[None, :] >= start
        gathered = []
        if panel == 0:
            x_own, c_own, *later = [
                jnp.where(below_cols, sent[source], 0.0) for source in range(PANELS + 1)
            ]
            gathered = [transposed(x_own)]
            x_cols = copied(x_own, "row").reshape(width, local)
        x_piece = lax.dynamic_slice_in_dim(x_cols, own, part, 0)
        gram_part = product(x_piece, x_cols, NT, highest)
        top_part = jnp.where(col_index == panel + 1, x_piece[:, :width], 0.0)
        summed = core_sum(jnp.concatenate([gram_part, top_part]))
        lines = copied(jnp.concatenate([summed.reshape(part, local), *gathered]), COL[0])
        sums = jnp.sum(lines[:, :part], axis=0).reshape(2 * part, width)
        if panel == 0:
            x_rows = both_cores(lines[:, part:]).reshape(width, local)
        u_part = product(x_rows, dense)
        shared = jnp.concatenate([sums, c_own.reshape(2 * part, width)])
        merged = jnp.concatenate(
            [
                jnp.broadcast_to(shared, (devices, *shared.shape)),
                u_part.reshape(devices, 2 * part, width),
            ],
            axis=1,
        )
        merged = exchange(merged, "row")
        gram = merged[:, :part].reshape(width, width)
        top = merged[:, part : 2 * part].reshape(width, width).T
        c_cols = merged[:, 2 * part : 4 * part].reshape(width, local)
        u_own = jnp.sum(merged[:, 4 * part :], axis=0).reshape(part, local)
        u_own = jnp.where(below_cols, u_own, 0.0)
        pair = transposed(jnp.stack([u_own, c_own]))
        pair = copied(pair, COL[0])
        upper, core = factor(gram, top)
        pair, upper, core = lax.optimization_barrier((pair, upper, core))
        u_rows, c_rows = join(both_cores(pair))
        lower = upper.T

        def with_top(x, index):
            head = jnp.where(index == panel + 1, lower, 0.0)
            return jnp.concatenate([x[:, :width] + head, x[:, width:]], axis=1)

        v_cols = with_top(x_cols, col_index)
        v_rows = with_top(x_rows, row_index)
        w_own = u_own + product(lax.dynamic_slice_in_dim(lower, own, part, 0), c_cols)
        w_rows = u_rows + product(lower, c_rows)
        parts = [product(w_own, v_cols, NT)]
        if not last:
            across = lax.dynamic_slice_in_dim(x_cols, own, part, 1).T
            parts += [
                jnp.where(col_index == panel + 1, w_own[:, :width], 0.0),
                jnp.where(col_index == panel + 2, w_own[:, :width], 0.0),
                jnp.where(col_index == panel + 2, across, 0.0),
            ]
        sums = jnp.sum(copied(core_sum(jnp.concatenate(parts)), COL[0]), axis=0)
        shared = jnp.concatenate([w_own.reshape(2 * part, width), sums[: 3 * part]])
        shared = copied(shared, "row")
        w_cols = shared[:, : 2 * part].reshape(width, local)
        inner = shared[:, 2 * part : 3 * part].reshape(width, width)
        middle = 0.5 * product(product(core, inner), core, NT)
        y_cols = product(core, w_cols) - product(middle, v_cols)
        y_rows = product(core, w_rows) - product(middle, v_rows)
        dense = dense - product(
            jnp.concatenate([y_rows, v_rows]), jnp.concatenate([v_cols, y_cols]), TN
        )
        corners.append(upper)
        if last:
            break

        def reduced(old, w_t, v, v_others, y_others):
            y = product(w_t, core, ((0,), (1,))) - product(v, middle, NT)
            both = jnp.concatenate([y, v], axis=1)
            return old - product(both, jnp.concatenate([v_others, y_others]))

        w_top = shared[:, 3 * part : 4 * part].reshape(width, width)
        w_next = shared[:, 4 * part :].reshape(width, width)
        w_next = lax.dynamic_slice_in_dim(w_next, own, part, 1)
        v_top = top + upper
        x_cols = reduced(c_cols, w_top, v_top, v_cols, y_cols)
        x_rows = reduced(c_rows, w_top, v_top, v_rows, y_rows)
        c_own = reduced(later[0], w_next, sums[3 * part :], v_cols, y_cols)
        x_cols = jnp.where(global_cols[None, :] >= start + width, x_cols, 0.0)
        x_rows = jnp.where(global_rows[None, :] >= start + width, x_rows, 0.0)
        c_own = jnp.where(global_cols[None, :] >= start + width, c_own, 0.0)
    slot_rows = offsets[:, None] < width
    slot_cols = offsets[None, :] < width
    for panel, upper in enumerate(corners):
        start = (panel + 1) * width
        pad = ((0, local - width), (0, local - width))
        at_cols = (col_index == panel) & slot_cols & (global_rows[:, None] >= start)
        new_cols = jnp.where(row_index == panel + 1, -jnp.pad(upper, pad), 0.0)
        dense = jnp.where(at_cols, new_cols, dense)
        at_rows = (row_index == panel) & slot_rows & (global_cols[None, :] >= start)
        new_rows = jnp.where(col_index == panel + 1, -jnp.pad(upper.T, pad), 0.0)
        dense = jnp.where(at_rows, new_rows, dense)
    return dense.reshape(matrix.shape)


def solution(mesh):
    split = Mesh(mesh.devices.reshape(mesh.shape["row"], 8, 2), ("row", "col_0", "col_1"))
    placed = (P(None, "row", None, COL),)
    return jax.shard_map(
        shards, mesh=split, in_specs=placed, out_specs=P(None, "row", None, COL), check_vma=False
    )
```

```python
import functools

import jax
import jax.numpy as jnp
from jax import lax
from jax.experimental import pallas as pl
from jax.experimental.pallas import tpu as pltpu
from jax.sharding import Mesh
from jax.sharding import PartitionSpec as P

PANELS = 2
COL = ("col_0", "col_1")

highest = lax.Precision.HIGHEST
high = lax.Precision.HIGH


def product(left, right, dims=((1,), (0,)), precision=high):
    return lax.dot_general(
        left, right, (dims, ((), ())), precision=precision, preferred_element_type=jnp.float32
    )


NT = ((1,), (1,))
TN = ((0,), (0,))
GROUP = 8


def row_of(tile, s):
    return jnp.broadcast_to(tile[s : s + 1, :], (8, 128))


class Elimination:
    def __init__(self, window, off, b):
        self.b, self.off, self.count = b, off, b // 8
        self.sublane = lax.broadcasted_iota(jnp.int32, (8, 128), 0)
        lanes = lax.broadcasted_iota(jnp.int32, (8, 128), 1)
        self.a = [window[8 * i : 8 * i + 8, :] for i in range(self.count)]
        self.e = [(lanes == self.sublane + 8 * i).astype(jnp.float32) for i in range(self.count)]
        zero = jnp.zeros((8, 128), jnp.float32)
        self.low = [zero] * self.count
        self.inv = [zero] * self.count

    def group(self, t):
        tiles = range(self.count)
        first = self.off + GROUP * t
        cols = [
            [jnp.broadcast_to(self.a[i][:, first + q : first + q + 1], (8, 128)) for i in tiles]
            for q in range(GROUP)
        ]
        for q in range(GROUP):
            inv = 1.0 / row_of(cols[q][t], q)
            here = self.sublane == q
            scale = [cols[q][i] * inv for i in tiles]
            scale[t] = jnp.where(here, 0.0, scale[t])
            for p in range(q + 1, GROUP):
                head = row_of(cols[p][t], q)
                for i in tiles:
                    cols[p][i] = cols[p][i] - scale[i] * head
            self.inv[t] = jnp.where(here, inv, self.inv[t])
            self.low[t] = jnp.where(here, self.e[t], self.low[t])
            row_a = row_of(self.a[t], q)
            row_e = row_of(self.e[t], q)
            for i in tiles:
                self.a[i] = self.a[i] - scale[i] * row_a
                self.e[i] = self.e[i] - scale[i] * row_e

    def inverse(self):
        inv = jnp.concatenate(self.inv, axis=0)
        return (jnp.concatenate(self.e, axis=0) * inv)[:, : self.b]

    def lower_inverse(self):
        inv = jnp.concatenate(self.inv, axis=0)
        return (jnp.concatenate(self.low, axis=0) * jnp.sqrt(inv))[:, : self.b]


def factor_kernel(g_ref, x_ref, r_ref, t_ref, aa, xb, wb, *, b):
    exact = functools.partial(product, precision=highest)
    n = g_ref.shape[0]
    count = n // b
    rows = lax.broadcasted_iota(jnp.int32, (n, n), 0)
    cols = lax.broadcasted_iota(jnp.int32, (n, n), 1)
    aa[:, :n] = g_ref[...]
    aa[:, n:] = (rows == cols).astype(jnp.float32)
    xb[:, :n] = x_ref[...]
    xb[:, n:] = jnp.zeros((n, n), jnp.float32)
    wb[...] = jnp.zeros((128, 2 * n), jnp.float32)
    lane = lax.broadcasted_iota(jnp.int32, (n, 128), 1)
    row = lax.broadcasted_iota(jnp.int32, (n, 128), 0)
    second = None
    for k in range(count + 1):
        lo, hi = k * b, (k + 1) * b
        win, off = lo // 128 * 128, lo % 128
        running = []
        if k < count:
            first = Elimination(aa[lo:hi, win : win + 128], off, b)
            running.append(first)
        if k > 0:
            second = Elimination(pivot, (lo - b) % 128, b)
            running.append(second)
        for t in range(b // 8):
            for one in running:
                one.group(t)
        if k < count:
            block = aa[lo:hi, :]
            if hi < n:
                wb[off : off + b, :] = exact(first.inverse(), block)
                keep = (lane[: n - hi] >= off) & (lane[: n - hi] < off + b)
                left = jnp.where(keep, aa[hi:, win : win + 128], 0.0)
                aa[hi:, :] = aa[hi:, :] - exact(left, wb[...])
            upper = exact(first.lower_inverse(), block)
            wide_row = lax.broadcasted_iota(jnp.int32, (b, 2 * n), 0) + lo
            wide_col = lax.broadcasted_iota(jnp.int32, (b, 2 * n), 1)
            upper = jnp.where(wide_col >= wide_row, upper, 0.0)
            upper = jnp.where(wide_col - n > wide_row, 0.0, upper)
            r_ref[lo:hi, :] = upper[:, :n]
        if k > 0:
            plo, phi = lo - b, lo
            pwin, poff = plo // 128 * 128, plo % 128
            xb[plo:phi, :] = exact(second.inverse(), pivot_row)
            keep = (lane >= poff) & (lane < poff + b) & ((row < plo) | (row >= phi))
            left = jnp.where(keep, xb[:, pwin : pwin + 128], 0.0)
            xb[...] = xb[...] - exact(left, xb[pwin : pwin + 128, :])
        if k < count:
            pivot_row = xb[lo:hi, :] + upper
            pivot = pivot_row[:, win : win + 128]
    t_ref[...] = xb[:, n:]


def factor(gram, top):
    n = gram.shape[0]
    square = jax.ShapeDtypeStruct((n, n), jnp.float32)
    return pl.pallas_call(
        functools.partial(factor_kernel, b=32),
        out_shape=(square, square),
        scratch_shapes=[
            pltpu.VMEM((n, 2 * n), jnp.float32),
            pltpu.VMEM((n, 2 * n), jnp.float32),
            pltpu.VMEM((128, 2 * n), jnp.float32),
        ],
        name="factor",
    )(gram, top)


def exchange(value, axis):
    return lax.all_to_all(value, axis, 0, 0, tiled=True)


def copied(value, axis):
    copies = jnp.broadcast_to(value, (lax.axis_size(axis), *value.shape))
    return exchange(copies, axis)


def transposed(value):
    rows = lax.axis_size("row")
    cols = lax.axis_size(COL)
    pairs = [(r * cols + c, c * rows + r) for r in range(rows) for c in range(cols)]
    return lax.ppermute(value, ("row", *COL), pairs)


def swapped(value):
    return lax.ppermute(value, COL[1], [(0, 1), (1, 0)])


def core_sum(value):
    return value + swapped(value)


def both_cores(lines):
    other = swapped(lines)
    second = lax.axis_index(COL[1]) == 1
    pair = [jnp.where(second, other, lines), jnp.where(second, lines, other)]
    return jnp.stack(pair, axis=1)


def join(parts):
    parts = parts.reshape(-1, *parts.shape[-3:])
    first, last = parts[:, 0], parts[:, 1]
    local = parts.shape[-1]
    return first.reshape(-1, local), last.reshape(-1, local)


def shards(matrix):
    row_blocks, width, _, _ = matrix.shape
    devices = lax.axis_size("row")
    row_index = lax.axis_index("row")
    col_index = lax.axis_index(COL)
    local = row_blocks * width
    part = width // devices
    dense = matrix.reshape(local, local)
    offsets = jnp.arange(local, dtype=jnp.int32)
    global_rows = (offsets // width * devices + row_index) * width + offsets % width
    global_cols = (offsets // width * devices + col_index) * width + offsets % width
    own = row_index * part
    corners = []
    sent = exchange(dense[:width].reshape(devices, part, local), "row")
    for panel in range(PANELS):
        start = (panel + 1) * width
        last = panel + 1 == PANELS
        below_cols = global_cols[None, :] >= start
        if panel == 0:
            x_own, c_own, *later = [
                jnp.where(below_cols, sent[source], 0.0) for source in range(PANELS + 1)
            ]
            x_rows = both_cores(copied(transposed(x_own), COL[0])).reshape(width, local)
        u_part = product(x_rows, dense)
        x_piece = lax.dynamic_slice_in_dim(x_rows, col_index * part, part, 0)
        gram_part = product(x_piece, x_rows, NT, highest)
        top_part = jnp.where(row_index == panel + 1, x_piece[:, :width], 0.0)
        shared = [gram_part, top_part, c_own.reshape(2 * part, width)]
        if panel == 0:
            shared.append(x_own.reshape(2 * part, width))
        shared = jnp.concatenate(shared)
        merged = jnp.concatenate(
            [
                jnp.broadcast_to(shared, (devices, *shared.shape)),
                u_part.reshape(devices, 2 * part, width),
            ],
            axis=1,
        )
        merged = exchange(merged, "row")
        sums = copied(jnp.sum(merged[:, : 2 * part], axis=0), COL)
        gram = sums[:, :part].reshape(width, width)
        top = sums[:, part:].reshape(width, width).T
        c_cols = merged[:, 2 * part : 4 * part].reshape(width, local)
        if panel == 0:
            x_cols = merged[:, 4 * part : 6 * part].reshape(width, local)
        u_own = jnp.sum(merged[:, -2 * part :], axis=0).reshape(part, local)
        u_own = jnp.where(below_cols, u_own, 0.0)
        pair = transposed(jnp.stack([u_own, c_own]))
        pair = copied(pair, COL[0])
        upper, core = factor(gram, top)
        pair, upper, core = lax.optimization_barrier((pair, upper, core))
        u_rows, c_rows = join(both_cores(pair))
        lower = upper.T

        def with_top(x, index):
            head = jnp.where(index == panel + 1, lower, 0.0)
            return jnp.concatenate([x[:, :width] + head, x[:, width:]], axis=1)

        v_cols = with_top(x_cols, col_index)
        v_rows = with_top(x_rows, row_index)
        w_own = u_own + product(lax.dynamic_slice_in_dim(lower, own, part, 0), c_cols)
        w_rows = u_rows + product(lower, c_rows)
        parts = [product(w_own, v_cols, NT)]
        if not last:
            across = lax.dynamic_slice_in_dim(x_cols, own, part, 1).T
            parts += [
                jnp.where(col_index == panel + 1, w_own[:, :width], 0.0),
                jnp.where(col_index == panel + 2, w_own[:, :width], 0.0),
                jnp.where(col_index == panel + 2, across, 0.0),
            ]
        if last:
            sums = jnp.sum(copied(parts[0], COL), axis=0)
        else:
            sums = jnp.sum(copied(core_sum(jnp.concatenate(parts)), COL[0]), axis=0)
        shared = jnp.concatenate([w_own.reshape(2 * part, width), sums[: 3 * part]])
        shared = copied(shared, "row")
        w_cols = shared[:, : 2 * part].reshape(width, local)
        inner = shared[:, 2 * part : 3 * part].reshape(width, width)
        middle = 0.5 * product(product(core, inner), core, NT)
        y_cols = product(core, w_cols) - product(middle, v_cols)
        y_rows = product(core, w_rows) - product(middle, v_rows)
        dense = dense - product(
            jnp.concatenate([y_rows, v_rows]), jnp.concatenate([v_cols, y_cols]), TN
        )
        corners.append(upper)
        if last:
            break

        def reduced(old, w_t, v, v_others, y_others):
            y = product(w_t, core, ((0,), (1,))) - product(v, middle, NT)
            both = jnp.concatenate([y, v], axis=1)
            return old - product(both, jnp.concatenate([v_others, y_others]))

        w_top = shared[:, 3 * part : 4 * part].reshape(width, width)
        w_next = shared[:, 4 * part :].reshape(width, width)
        w_next = lax.dynamic_slice_in_dim(w_next, own, part, 1)
        v_top = top + upper
        x_cols = reduced(c_cols, w_top, v_top, v_cols, y_cols)
        x_rows = reduced(c_rows, w_top, v_top, v_rows, y_rows)
        c_own = reduced(later[0], w_next, sums[3 * part :], v_cols, y_cols)
        x_cols = jnp.where(global_cols[None, :] >= start + width, x_cols, 0.0)
        x_rows = jnp.where(global_rows[None, :] >= start + width, x_rows, 0.0)
        c_own = jnp.where(global_cols[None, :] >= start + width, c_own, 0.0)
    slot_rows = offsets[:, None] < width
    slot_cols = offsets[None, :] < width
    for panel, upper in enumerate(corners):
        start = (panel + 1) * width
        pad = ((0, local - width), (0, local - width))
        at_cols = (col_index == panel) & slot_cols & (global_rows[:, None] >= start)
        new_cols = jnp.where(row_index == panel + 1, -jnp.pad(upper, pad), 0.0)
        dense = jnp.where(at_cols, new_cols, dense)
        at_rows = (row_index == panel) & slot_rows & (global_cols[None, :] >= start)
        new_rows = jnp.where(col_index == panel + 1, -jnp.pad(upper.T, pad), 0.0)
        dense = jnp.where(at_rows, new_rows, dense)
    return dense.reshape(matrix.shape)


def solution(mesh):
    split = Mesh(mesh.devices.reshape(mesh.shape["row"], 8, 2), ("row", "col_0", "col_1"))
    placed = (P(None, "row", None, COL),)
    return jax.shard_map(
        shards, mesh=split, in_specs=placed, out_specs=P(None, "row", None, COL), check_vma=False
    )
```

```python
import functools

import jax
import jax.numpy as jnp
from jax import lax
from jax.experimental import pallas as pl
from jax.experimental.layout import Layout, with_layout_constraint
from jax.experimental.pallas import tpu as pltpu
from jax.sharding import Mesh
from jax.sharding import PartitionSpec as P

PANELS = 2
COL = ("col_0", "col_1")

highest = lax.Precision.HIGHEST
high = lax.Precision.HIGH


def product(left, right, dims=((1,), (0,)), precision=high):
    return lax.dot_general(
        left, right, (dims, ((), ())), precision=precision, preferred_element_type=jnp.float32
    )


NT = ((1,), (1,))
TN = ((0,), (0,))
GROUP = 8


def row_of(tile, s):
    return jnp.broadcast_to(tile[s : s + 1, :], (8, 128))


class Elimination:
    def __init__(self, window, off, b):
        self.b, self.off, self.count = b, off, b // 8
        self.sublane = lax.broadcasted_iota(jnp.int32, (8, 128), 0)
        lanes = lax.broadcasted_iota(jnp.int32, (8, 128), 1)
        self.a = [window[8 * i : 8 * i + 8, :] for i in range(self.count)]
        self.e = [(lanes == self.sublane + 8 * i).astype(jnp.float32) for i in range(self.count)]
        zero = jnp.zeros((8, 128), jnp.float32)
        self.low = [zero] * self.count
        self.inv = [zero] * self.count

    def group(self, t):
        tiles = range(self.count)
        first = self.off + GROUP * t
        cols = [
            [jnp.broadcast_to(self.a[i][:, first + q : first + q + 1], (8, 128)) for i in tiles]
            for q in range(GROUP)
        ]
        for q in range(GROUP):
            inv = 1.0 / row_of(cols[q][t], q)
            here = self.sublane == q
            scale = [cols[q][i] * inv for i in tiles]
            scale[t] = jnp.where(here, 0.0, scale[t])
            for p in range(q + 1, GROUP):
                head = row_of(cols[p][t], q)
                for i in tiles:
                    cols[p][i] = cols[p][i] - scale[i] * head
            self.inv[t] = jnp.where(here, inv, self.inv[t])
            self.low[t] = jnp.where(here, self.e[t], self.low[t])
            row_a = row_of(self.a[t], q)
            row_e = row_of(self.e[t], q)
            for i in tiles:
                self.a[i] = self.a[i] - scale[i] * row_a
                self.e[i] = self.e[i] - scale[i] * row_e

    def inverse(self):
        inv = jnp.concatenate(self.inv, axis=0)
        return (jnp.concatenate(self.e, axis=0) * inv)[:, : self.b]

    def lower_inverse(self):
        inv = jnp.concatenate(self.inv, axis=0)
        return (jnp.concatenate(self.low, axis=0) * jnp.sqrt(inv))[:, : self.b]


def factor_kernel(pieces_ref, r_ref, l_ref, t_ref, aa, xb, wb, *, b):
    exact = functools.partial(product, precision=highest)
    n = r_ref.shape[0]
    part = pieces_ref.shape[1] // 2
    count = n // b
    rows = lax.broadcasted_iota(jnp.int32, (n, n), 0)
    cols = lax.broadcasted_iota(jnp.int32, (n, n), 1)
    for i in range(n // part):
        aa[part * i : part * i + part, :n] = pieces_ref[i, :part, :]
        xb[part * i : part * i + part, n:] = pieces_ref[i, part:, :]
    aa[:, n:] = (rows == cols).astype(jnp.float32)
    xb[:, :n] = xb[:, n:].T
    xb[:, n:] = jnp.zeros((n, n), jnp.float32)
    wb[...] = jnp.zeros((128, 2 * n), jnp.float32)
    lane = lax.broadcasted_iota(jnp.int32, (n, 128), 1)
    row = lax.broadcasted_iota(jnp.int32, (n, 128), 0)
    second = None
    for k in range(count + 1):
        lo, hi = k * b, (k + 1) * b
        win, off = lo // 128 * 128, lo % 128
        running = []
        if k < count:
            first = Elimination(aa[lo:hi, win : win + 128], off, b)
            running.append(first)
        if k > 0:
            second = Elimination(pivot, (lo - b) % 128, b)
            running.append(second)
        for t in range(b // 8):
            for one in running:
                one.group(t)
        if k < count:
            block = aa[lo:hi, :]
            if hi < n:
                wb[off : off + b, :] = exact(first.inverse(), block)
                keep = (lane[: n - hi] >= off) & (lane[: n - hi] < off + b)
                left = jnp.where(keep, aa[hi:, win : win + 128], 0.0)
                aa[hi:, :] = aa[hi:, :] - exact(left, wb[...])
            upper = exact(first.lower_inverse(), block)
            wide_row = lax.broadcasted_iota(jnp.int32, (b, 2 * n), 0) + lo
            wide_col = lax.broadcasted_iota(jnp.int32, (b, 2 * n), 1)
            upper = jnp.where(wide_col >= wide_row, upper, 0.0)
            upper = jnp.where(wide_col - n > wide_row, 0.0, upper)
            r_ref[lo:hi, :] = upper[:, :n]
        if k > 0:
            plo, phi = lo - b, lo
            pwin, poff = plo // 128 * 128, plo % 128
            xb[plo:phi, :] = exact(second.inverse(), pivot_row)
            keep = (lane >= poff) & (lane < poff + b) & ((row < plo) | (row >= phi))
            left = jnp.where(keep, xb[:, pwin : pwin + 128], 0.0)
            xb[...] = xb[...] - exact(left, xb[pwin : pwin + 128, :])
        if k < count:
            pivot_row = xb[lo:hi, :] + upper
            pivot = pivot_row[:, win : win + 128]
    l_ref[...] = r_ref[...].T
    t_ref[...] = xb[:, n:]


def factor(pieces):
    n = pieces.shape[-1]
    square = jax.ShapeDtypeStruct((n, n), jnp.float32)
    return pl.pallas_call(
        functools.partial(factor_kernel, b=32),
        out_shape=(square, square, square),
        scratch_shapes=[
            pltpu.VMEM((n, 2 * n), jnp.float32),
            pltpu.VMEM((n, 2 * n), jnp.float32),
            pltpu.VMEM((128, 2 * n), jnp.float32),
        ],
        name="factor",
    )(pieces)


def exchange(value, axis):
    return lax.all_to_all(value, axis, 0, 0, tiled=True)


def copied(value, axis):
    copies = jnp.broadcast_to(value, (lax.axis_size(axis), *value.shape))
    return exchange(copies, axis)


def row_major(value):
    return with_layout_constraint(value, Layout(major_to_minor=tuple(range(value.ndim))))


def transposed(value):
    rows = lax.axis_size("row")
    cols = lax.axis_size(COL)
    pairs = [(r * cols + c, c * rows + r) for r in range(rows) for c in range(cols)]
    return lax.ppermute(row_major(value), ("row", *COL), pairs)


def swapped(value):
    return lax.ppermute(value, COL[1], [(0, 1), (1, 0)])


def core_sum(value):
    return value + swapped(value)


def both_cores(lines):
    other = swapped(lines)
    second = lax.axis_index(COL[1]) == 1
    pair = [jnp.where(second, other, lines), jnp.where(second, lines, other)]
    return jnp.stack(pair, axis=1)


def join(parts):
    parts = parts.reshape(-1, *parts.shape[-3:])
    first, last = parts[:, 0], parts[:, 1]
    local = parts.shape[-1]
    return first.reshape(-1, local), last.reshape(-1, local)


def shards(matrix):
    row_blocks, width, _, _ = matrix.shape
    devices = lax.axis_size("row")
    row_index = lax.axis_index("row")
    col_index = lax.axis_index(COL)
    local = row_blocks * width
    part = width // devices
    dense = matrix.reshape(local, local)
    offsets = jnp.arange(local, dtype=jnp.int32)
    global_rows = (offsets // width * devices + row_index) * width + offsets % width
    global_cols = (offsets // width * devices + col_index) * width + offsets % width
    own = row_index * part
    corners = []
    sent = exchange(dense[:width].reshape(devices, part, local), "row")
    for panel in range(PANELS):
        start = (panel + 1) * width
        last = panel + 1 == PANELS
        below_cols = global_cols[None, :] >= start
        if panel == 0:
            x_own, c_own, *later = [
                jnp.where(below_cols, sent[source], 0.0) for source in range(PANELS + 1)
            ]
            x_rows = both_cores(copied(transposed(x_own), COL[0])).reshape(width, local)
        u_part = product(x_rows, dense)
        x_piece = lax.dynamic_slice_in_dim(x_rows, col_index * part, part, 0)
        gram_part = product(x_piece, x_rows, NT, highest)
        top_part = jnp.where(row_index == panel + 1, x_piece[:, :width], 0.0)
        shared = [gram_part, top_part, c_own.reshape(2 * part, width)]
        if panel == 0:
            shared.append(x_own.reshape(2 * part, width))
        shared = jnp.concatenate(shared)
        merged = jnp.concatenate(
            [
                jnp.broadcast_to(shared, (devices, *shared.shape)),
                u_part.reshape(devices, 2 * part, width),
            ],
            axis=1,
        )
        merged = exchange(merged, "row")
        sums = copied(jnp.sum(merged[:, : 2 * part], axis=0), COL)
        pieces = sums
        c_cols = merged[:, 2 * part : 4 * part].reshape(width, local)
        if panel == 0:
            x_cols = merged[:, 4 * part : 6 * part].reshape(width, local)
        u_own = jnp.sum(merged[:, -2 * part :], axis=0).reshape(part, local)
        u_own = jnp.where(below_cols, u_own, 0.0)
        pair = transposed(jnp.stack([u_own, c_own]))
        pair = copied(pair, COL[0])
        factors = factor(pieces)
        pair, (upper, lower, core) = lax.optimization_barrier((pair, factors))
        u_rows, c_rows = join(both_cores(pair))

        def with_top(x, index):
            head = jnp.where(index == panel + 1, lower, 0.0)
            return jnp.concatenate([x[:, :width] + head, x[:, width:]], axis=1)

        v_cols = with_top(x_cols, col_index)
        v_rows = with_top(x_rows, row_index)
        w_own = u_own + product(lax.dynamic_slice_in_dim(lower, own, part, 0), c_cols)
        w_rows = u_rows + product(lower, c_rows)
        parts = [product(w_own, v_cols, NT)]
        if not last:
            across = lax.dynamic_slice_in_dim(x_cols[:, :width].T, own, part, 0)
            parts += [
                jnp.where(col_index == panel + 1, w_own[:, :width], 0.0),
                jnp.where(col_index == panel + 2, w_own[:, :width], 0.0),
                jnp.where(col_index == panel + 2, across, 0.0),
            ]
        if last:
            sums = jnp.sum(copied(parts[0], COL), axis=0)
        else:
            sums = jnp.sum(copied(core_sum(row_major(jnp.concatenate(parts))), COL[0]), axis=0)
        shared = jnp.concatenate([w_own.reshape(2 * part, width), sums[: 3 * part]])
        shared = copied(shared, "row")
        w_cols = shared[:, : 2 * part].reshape(width, local)
        inner = shared[:, 2 * part : 3 * part].reshape(width, width)
        middle = 0.5 * product(product(core, inner), core, NT)
        y_cols = product(core, w_cols) - product(middle, v_cols)
        y_rows = product(core, w_rows) - product(middle, v_rows)
        dense = dense - product(
            jnp.concatenate([y_rows, v_rows]), jnp.concatenate([v_cols, y_cols]), TN
        )
        corners.append(upper)
        if last:
            break

        def y_of(w_t, v):
            return product(w_t, core, ((0,), (1,))) - product(v, middle, NT)

        def reduced(old, y, v, v_others, y_others):
            both = jnp.concatenate([y, v], axis=1)
            return old - product(both, jnp.concatenate([v_others, y_others]))

        w_top = shared[:, 3 * part : 4 * part].reshape(width, width)
        w_next = shared[:, 4 * part :].reshape(width, width)
        v_top = pieces[:, part:].reshape(width, width).T + upper
        y_top = y_of(w_top, v_top)
        v_next = sums[3 * part :]
        y_next = lax.dynamic_slice_in_dim(product(w_next, core, ((0,), (1,))), own, part, 0)
        y_next = y_next - product(v_next, middle, NT)
        x_cols = reduced(c_cols, y_top, v_top, v_cols, y_cols)
        x_rows = reduced(c_rows, y_top, v_top, v_rows, y_rows)
        c_own = reduced(later[0], y_next, v_next, v_cols, y_cols)
        x_cols = jnp.where(global_cols[None, :] >= start + width, x_cols, 0.0)
        x_rows = jnp.where(global_rows[None, :] >= start + width, x_rows, 0.0)
        c_own = jnp.where(global_cols[None, :] >= start + width, c_own, 0.0)
    slot_rows = offsets[:, None] < width
    slot_cols = offsets[None, :] < width
    for panel, upper in enumerate(corners):
        start = (panel + 1) * width
        pad = ((0, local - width), (0, local - width))
        at_cols = (col_index == panel) & slot_cols & (global_rows[:, None] >= start)
        new_cols = jnp.where(row_index == panel + 1, -jnp.pad(upper, pad), 0.0)
        dense = jnp.where(at_cols, new_cols, dense)
        at_rows = (row_index == panel) & slot_rows & (global_cols[None, :] >= start)
        new_rows = jnp.where(col_index == panel + 1, -jnp.pad(upper.T, pad), 0.0)
        dense = jnp.where(at_rows, new_rows, dense)
    return dense.reshape(matrix.shape)


def solution(mesh):
    split = Mesh(mesh.devices.reshape(mesh.shape["row"], 8, 2), ("row", "col_0", "col_1"))
    placed = (P(None, "row", None, COL),)
    return jax.shard_map(
        shards, mesh=split, in_specs=placed, out_specs=P(None, "row", None, COL), check_vma=False
    )
```

```python
import functools

import jax
import jax.numpy as jnp
from jax import lax
from jax.experimental import pallas as pl
from jax.experimental.layout import Layout, with_layout_constraint
from jax.experimental.pallas import tpu as pltpu
from jax.sharding import Mesh
from jax.sharding import PartitionSpec as P

PANELS = 2
COL = ("col_0", "col_1")

highest = lax.Precision.HIGHEST
high = lax.Precision.HIGH


def product(left, right, dims=((1,), (0,)), precision=high):
    return lax.dot_general(
        left, right, (dims, ((), ())), precision=precision, preferred_element_type=jnp.float32
    )


NT = ((1,), (1,))
TN = ((0,), (0,))
GROUP = 8


def row_of(tile, s):
    return jnp.broadcast_to(tile[s : s + 1, :], (8, 128))


class Elimination:
    def __init__(self, window, off, b):
        self.b, self.off, self.count = b, off, b // 8
        self.sublane = lax.broadcasted_iota(jnp.int32, (8, 128), 0)
        lanes = lax.broadcasted_iota(jnp.int32, (8, 128), 1)
        self.a = [window[8 * i : 8 * i + 8, :] for i in range(self.count)]
        self.e = [(lanes == self.sublane + 8 * i).astype(jnp.float32) for i in range(self.count)]
        zero = jnp.zeros((8, 128), jnp.float32)
        self.low = [zero] * self.count
        self.inv = [zero] * self.count

    def group(self, t):
        tiles = range(self.count)
        first = self.off + GROUP * t
        cols = [
            [jnp.broadcast_to(self.a[i][:, first + q : first + q + 1], (8, 128)) for i in tiles]
            for q in range(GROUP)
        ]
        for q in range(GROUP):
            inv = 1.0 / row_of(cols[q][t], q)
            here = self.sublane == q
            scale = [cols[q][i] * inv for i in tiles]
            scale[t] = jnp.where(here, 0.0, scale[t])
            for p in range(q + 1, GROUP):
                head = row_of(cols[p][t], q)
                for i in tiles:
                    cols[p][i] = cols[p][i] - scale[i] * head
            self.inv[t] = jnp.where(here, inv, self.inv[t])
            self.low[t] = jnp.where(here, self.e[t], self.low[t])
            row_a = row_of(self.a[t], q)
            row_e = row_of(self.e[t], q)
            for i in tiles:
                self.a[i] = self.a[i] - scale[i] * row_a
                self.e[i] = self.e[i] - scale[i] * row_e

    def inverse(self):
        inv = jnp.concatenate(self.inv, axis=0)
        return (jnp.concatenate(self.e, axis=0) * inv)[:, : self.b]

    def lower_inverse(self):
        inv = jnp.concatenate(self.inv, axis=0)
        return (jnp.concatenate(self.low, axis=0) * jnp.sqrt(inv))[:, : self.b]


def factor_kernel(pieces_ref, r_ref, l_ref, t_ref, aa, xb, wb, *, b):
    exact = functools.partial(product, precision=highest)
    n = r_ref.shape[0]
    part = pieces_ref.shape[1] // 2
    count = n // b
    rows = lax.broadcasted_iota(jnp.int32, (n, n), 0)
    cols = lax.broadcasted_iota(jnp.int32, (n, n), 1)
    for i in range(n // part):
        aa[part * i : part * i + part, :n] = pieces_ref[i, :part, :]
        xb[part * i : part * i + part, n:] = pieces_ref[i, part:, :]
    aa[:, n:] = (rows == cols).astype(jnp.float32)
    xb[:, :n] = xb[:, n:].T
    xb[:, n:] = jnp.zeros((n, n), jnp.float32)
    wb[...] = jnp.zeros((128, 2 * n), jnp.float32)
    lane = lax.broadcasted_iota(jnp.int32, (n, 128), 1)
    row = lax.broadcasted_iota(jnp.int32, (n, 128), 0)
    second = None
    for k in range(count + 1):
        lo, hi = k * b, (k + 1) * b
        win, off = lo // 128 * 128, lo % 128
        running = []
        if k < count:
            first = Elimination(aa[lo:hi, win : win + 128], off, b)
            running.append(first)
        if k > 0:
            second = Elimination(pivot, (lo - b) % 128, b)
            running.append(second)
        for t in range(b // 8):
            for one in running:
                one.group(t)
        if k < count:
            block = aa[lo:hi, :]
            if hi < n:
                wb[off : off + b, :] = exact(first.inverse(), block)
                keep = (lane[: n - hi] >= off) & (lane[: n - hi] < off + b)
                left = jnp.where(keep, aa[hi:, win : win + 128], 0.0)
                aa[hi:, :] = aa[hi:, :] - exact(left, wb[...])
            upper = exact(first.lower_inverse(), block)
            wide_row = lax.broadcasted_iota(jnp.int32, (b, 2 * n), 0) + lo
            wide_col = lax.broadcasted_iota(jnp.int32, (b, 2 * n), 1)
            upper = jnp.where(wide_col >= wide_row, upper, 0.0)
            upper = jnp.where(wide_col - n > wide_row, 0.0, upper)
            r_ref[lo:hi, :] = upper[:, :n]
        if k > 0:
            plo, phi = lo - b, lo
            pwin, poff = plo // 128 * 128, plo % 128
            xb[plo:phi, :] = exact(second.inverse(), pivot_row)
            keep = (lane >= poff) & (lane < poff + b) & ((row < plo) | (row >= phi))
            left = jnp.where(keep, xb[:, pwin : pwin + 128], 0.0)
            xb[...] = xb[...] - exact(left, xb[pwin : pwin + 128, :])
        if k < count:
            pivot_row = xb[lo:hi, :] + upper
            pivot = pivot_row[:, win : win + 128]
    l_ref[...] = r_ref[...].T
    t_ref[...] = xb[:, n:]


def factor(pieces):
    n = pieces.shape[-1]
    square = jax.ShapeDtypeStruct((n, n), jnp.float32)
    return pl.pallas_call(
        functools.partial(factor_kernel, b=32),
        out_shape=(square, square, square),
        scratch_shapes=[
            pltpu.VMEM((n, 2 * n), jnp.float32),
            pltpu.VMEM((n, 2 * n), jnp.float32),
            pltpu.VMEM((128, 2 * n), jnp.float32),
        ],
        name="factor",
    )(pieces)


def exchange(value, axis):
    return lax.all_to_all(value, axis, 0, 0, tiled=True)


def copied(value, axis):
    copies = jnp.broadcast_to(value, (lax.axis_size(axis), *value.shape))
    return exchange(copies, axis)


def row_major(value):
    return with_layout_constraint(value, Layout(major_to_minor=tuple(range(value.ndim))))


def transposed(value):
    rows = lax.axis_size("row")
    cols = lax.axis_size(COL)
    pairs = [(r * cols + c, c * rows + r) for r in range(rows) for c in range(cols)]
    return lax.ppermute(row_major(value), ("row", *COL), pairs)


def swapped(value):
    return lax.ppermute(value, COL[1], [(0, 1), (1, 0)])


def core_sum(value):
    return value + swapped(value)


def both_cores(lines):
    other = swapped(lines)
    second = lax.axis_index(COL[1]) == 1
    pair = [jnp.where(second, other, lines), jnp.where(second, lines, other)]
    return jnp.stack(pair, axis=1)


def join(parts):
    parts = parts.reshape(-1, *parts.shape[-3:])
    first, last = parts[:, 0], parts[:, 1]
    local = parts.shape[-1]
    return first.reshape(-1, local), last.reshape(-1, local)


def shards(matrix):
    row_blocks, width, _, _ = matrix.shape
    devices = lax.axis_size("row")
    row_index = lax.axis_index("row")
    col_index = lax.axis_index(COL)
    local = row_blocks * width
    part = width // devices
    dense = matrix.reshape(local, local)
    offsets = jnp.arange(local, dtype=jnp.int32)
    global_rows = (offsets // width * devices + row_index) * width + offsets % width
    global_cols = (offsets // width * devices + col_index) * width + offsets % width
    own = row_index * part
    corners = []
    sent = exchange(dense[:width].reshape(devices, part, local), "row")
    for panel in range(PANELS):
        start = (panel + 1) * width
        last = panel + 1 == PANELS
        below_cols = global_cols[None, :] >= start
        if panel == 0:
            x_own, c_own, *later = [
                jnp.where(below_cols, sent[source], 0.0) for source in range(PANELS + 1)
            ]
            x_rows = both_cores(copied(transposed(x_own), COL[0])).reshape(width, local)
        u_part = product(x_rows, dense)
        x_piece = lax.dynamic_slice_in_dim(x_rows, col_index * part, part, 0)
        gram_part = product(x_piece, x_rows, NT, highest)
        top_part = jnp.where(row_index == panel + 1, x_piece[:, :width], 0.0)
        shared = [gram_part, top_part, c_own.reshape(2 * part, width)]
        if panel == 0:
            shared.append(x_own.reshape(2 * part, width))
        shared = jnp.concatenate(shared)
        merged = jnp.concatenate(
            [
                jnp.broadcast_to(shared, (devices, *shared.shape)),
                u_part.reshape(devices, 2 * part, width),
            ],
            axis=1,
        )
        merged = exchange(merged, "row")
        sums = copied(jnp.sum(merged[:, : 2 * part], axis=0), COL)
        pieces = sums
        c_cols = merged[:, 2 * part : 4 * part].reshape(width, local)
        if panel == 0:
            x_cols = merged[:, 4 * part : 6 * part].reshape(width, local)
        u_own = jnp.sum(merged[:, -2 * part :], axis=0).reshape(part, local)
        u_own = jnp.where(below_cols, u_own, 0.0)
        if last:
            upper, lower, core = factor(pieces)
        else:
            pair = transposed(jnp.stack([u_own, c_own]))
            pair = copied(pair, COL[0])
            factors = factor(pieces)
            pair, (upper, lower, core) = lax.optimization_barrier((pair, factors))
            u_rows, c_rows = join(both_cores(pair))

        def with_top(x, index):
            head = jnp.where(index == panel + 1, lower, 0.0)
            return jnp.concatenate([x[:, :width] + head, x[:, width:]], axis=1)

        v_cols = with_top(x_cols, col_index)
        v_rows = with_top(x_rows, row_index)
        w_own = u_own + product(lax.dynamic_slice_in_dim(lower, own, part, 0), c_cols)
        parts = [product(w_own, v_cols, NT)]
        if last:
            turned = transposed(w_own)
            own_sum = core_sum(row_major(parts[0])).reshape(part // 2, local)
            lines = copied(jnp.concatenate([turned, own_sum]), COL[0])
            sums = jnp.sum(lines[:, part:], axis=0).reshape(part, width)
            w_rows = both_cores(lines[:, :part]).reshape(width, local)
        else:
            w_rows = u_rows + product(lower, c_rows)
            across = lax.dynamic_slice_in_dim(x_cols[:, :width].T, own, part, 0)
            parts += [
                jnp.where(col_index == panel + 1, w_own[:, :width], 0.0),
                jnp.where(col_index == panel + 2, w_own[:, :width], 0.0),
                jnp.where(col_index == panel + 2, across, 0.0),
            ]
            sums = core_sum(row_major(jnp.concatenate(parts)))
            sums = jnp.sum(copied(sums, COL[0]), axis=0)
        shared = jnp.concatenate([w_own.reshape(2 * part, width), sums[: 3 * part]])
        shared = copied(shared, "row")
        w_cols = shared[:, : 2 * part].reshape(width, local)
        inner = shared[:, 2 * part : 3 * part].reshape(width, width)
        middle = 0.5 * product(product(core, inner), core, NT)
        y_cols = product(core, w_cols) - product(middle, v_cols)
        y_rows = product(core, w_rows) - product(middle, v_rows)
        dense = dense - product(
            jnp.concatenate([y_rows, v_rows]), jnp.concatenate([v_cols, y_cols]), TN
        )
        corners.append(upper)
        if last:
            break

        def y_of(w_t, v):
            return product(w_t, core, ((0,), (1,))) - product(v, middle, NT)

        def reduced(old, y, v, v_others, y_others):
            both = jnp.concatenate([y, v], axis=1)
            return old - product(both, jnp.concatenate([v_others, y_others]))

        w_top = shared[:, 3 * part : 4 * part].reshape(width, width)
        w_next = shared[:, 4 * part :].reshape(width, width)
        v_top = pieces[:, part:].reshape(width, width).T + upper
        y_top = y_of(w_top, v_top)
        v_next = sums[3 * part :]
        y_next = lax.dynamic_slice_in_dim(product(w_next, core, ((0,), (1,))), own, part, 0)
        y_next = y_next - product(v_next, middle, NT)
        x_cols = reduced(c_cols, y_top, v_top, v_cols, y_cols)
        x_rows = reduced(c_rows, y_top, v_top, v_rows, y_rows)
        c_own = reduced(later[0], y_next, v_next, v_cols, y_cols)
        x_cols = jnp.where(global_cols[None, :] >= start + width, x_cols, 0.0)
        x_rows = jnp.where(global_rows[None, :] >= start + width, x_rows, 0.0)
        c_own = jnp.where(global_cols[None, :] >= start + width, c_own, 0.0)
    slot_rows = offsets[:, None] < width
    slot_cols = offsets[None, :] < width
    for panel, upper in enumerate(corners):
        start = (panel + 1) * width
        pad = ((0, local - width), (0, local - width))
        at_cols = (col_index == panel) & slot_cols & (global_rows[:, None] >= start)
        new_cols = jnp.where(row_index == panel + 1, -jnp.pad(upper, pad), 0.0)
        dense = jnp.where(at_cols, new_cols, dense)
        at_rows = (row_index == panel) & slot_rows & (global_cols[None, :] >= start)
        new_rows = jnp.where(col_index == panel + 1, -jnp.pad(upper.T, pad), 0.0)
        dense = jnp.where(at_rows, new_rows, dense)
    return dense.reshape(matrix.shape)


def solution(mesh):
    split = Mesh(mesh.devices.reshape(mesh.shape["row"], 8, 2), ("row", "col_0", "col_1"))
    placed = (P(None, "row", None, COL),)
    return jax.shard_map(
        shards, mesh=split, in_specs=placed, out_specs=P(None, "row", None, COL), check_vma=False
    )
```

```python
import functools

import jax
import jax.numpy as jnp
from jax import lax
from jax.experimental import pallas as pl
from jax.experimental.layout import Layout, with_layout_constraint
from jax.experimental.pallas import tpu as pltpu
from jax.sharding import Mesh
from jax.sharding import PartitionSpec as P

PANELS = 2
COL = ("col_0", "col_1")

highest = lax.Precision.HIGHEST
high = lax.Precision.HIGH


def product(left, right, dims=((1,), (0,)), precision=high):
    return lax.dot_general(
        left, right, (dims, ((), ())), precision=precision, preferred_element_type=jnp.float32
    )


NT = ((1,), (1,))
TN = ((0,), (0,))
GROUP = 8


def row_of(tile, s):
    return jnp.broadcast_to(tile[s : s + 1, :], (8, 128))


class Elimination:
    def __init__(self, window, off, b):
        self.b, self.off, self.count = b, off, b // 8
        self.sublane = lax.broadcasted_iota(jnp.int32, (8, 128), 0)
        lanes = lax.broadcasted_iota(jnp.int32, (8, 128), 1)
        self.a = [window[8 * i : 8 * i + 8, :] for i in range(self.count)]
        self.e = [(lanes == self.sublane + 8 * i).astype(jnp.float32) for i in range(self.count)]
        zero = jnp.zeros((8, 128), jnp.float32)
        self.low = [zero] * self.count
        self.inv = [zero] * self.count

    def group(self, t):
        tiles = range(self.count)
        first = self.off + GROUP * t
        cols = [
            [jnp.broadcast_to(self.a[i][:, first + q : first + q + 1], (8, 128)) for i in tiles]
            for q in range(GROUP)
        ]
        for q in range(GROUP):
            inv = 1.0 / row_of(cols[q][t], q)
            here = self.sublane == q
            scale = [cols[q][i] * inv for i in tiles]
            scale[t] = jnp.where(here, 0.0, scale[t])
            for p in range(q + 1, GROUP):
                head = row_of(cols[p][t], q)
                for i in tiles:
                    cols[p][i] = cols[p][i] - scale[i] * head
            self.inv[t] = jnp.where(here, inv, self.inv[t])
            self.low[t] = jnp.where(here, self.e[t], self.low[t])
            row_a = row_of(self.a[t], q)
            row_e = row_of(self.e[t], q)
            for i in tiles:
                self.a[i] = self.a[i] - scale[i] * row_a
                self.e[i] = self.e[i] - scale[i] * row_e

    def inverse(self):
        inv = jnp.concatenate(self.inv, axis=0)
        return (jnp.concatenate(self.e, axis=0) * inv)[:, : self.b]

    def lower_inverse(self):
        inv = jnp.concatenate(self.inv, axis=0)
        return (jnp.concatenate(self.low, axis=0) * jnp.sqrt(inv))[:, : self.b]


def factor_kernel(pieces_ref, r_ref, l_ref, t_ref, aa, xb, wb, *, b):
    exact = functools.partial(product, precision=highest)
    n = r_ref.shape[0]
    part = pieces_ref.shape[1] // 2
    count = n // b
    rows = lax.broadcasted_iota(jnp.int32, (n, n), 0)
    cols = lax.broadcasted_iota(jnp.int32, (n, n), 1)
    for i in range(n // part):
        aa[part * i : part * i + part, :n] = pieces_ref[i, :part, :]
        xb[part * i : part * i + part, n:] = pieces_ref[i, part:, :]
    aa[:, n:] = (rows == cols).astype(jnp.float32)
    xb[:, :n] = xb[:, n:].T
    xb[:, n:] = jnp.zeros((n, n), jnp.float32)
    wb[...] = jnp.zeros((128, 2 * n), jnp.float32)
    lane = lax.broadcasted_iota(jnp.int32, (n, 128), 1)
    row = lax.broadcasted_iota(jnp.int32, (n, 128), 0)
    second = None
    for k in range(count + 1):
        lo, hi = k * b, (k + 1) * b
        win, off = lo // 128 * 128, lo % 128
        running = []
        if k < count:
            first = Elimination(aa[lo:hi, win : win + 128], off, b)
            running.append(first)
        if k > 0:
            second = Elimination(pivot, (lo - b) % 128, b)
            running.append(second)
        for t in range(b // 8):
            for one in running:
                one.group(t)
        if k < count:
            block = aa[lo:hi, :]
            if hi < n:
                wb[off : off + b, :] = exact(first.inverse(), block)
                keep = (lane[: n - hi] >= off) & (lane[: n - hi] < off + b)
                left = jnp.where(keep, aa[hi:, win : win + 128], 0.0)
                aa[hi:, :] = aa[hi:, :] - exact(left, wb[...])
            upper = exact(first.lower_inverse(), block)
            wide_row = lax.broadcasted_iota(jnp.int32, (b, 2 * n), 0) + lo
            wide_col = lax.broadcasted_iota(jnp.int32, (b, 2 * n), 1)
            upper = jnp.where(wide_col >= wide_row, upper, 0.0)
            upper = jnp.where(wide_col - n > wide_row, 0.0, upper)
            r_ref[lo:hi, :] = upper[:, :n]
        if k > 0:
            plo, phi = lo - b, lo
            pwin, poff = plo // 128 * 128, plo % 128
            xb[plo:phi, :] = exact(second.inverse(), pivot_row)
            keep = (lane >= poff) & (lane < poff + b) & ((row < plo) | (row >= phi))
            left = jnp.where(keep, xb[:, pwin : pwin + 128], 0.0)
            xb[...] = xb[...] - exact(left, xb[pwin : pwin + 128, :])
        if k < count:
            pivot_row = xb[lo:hi, :] + upper
            pivot = pivot_row[:, win : win + 128]
    l_ref[...] = r_ref[...].T
    t_ref[...] = xb[:, n:]


def factor(pieces):
    n = pieces.shape[-1]
    square = jax.ShapeDtypeStruct((n, n), jnp.float32)
    return pl.pallas_call(
        functools.partial(factor_kernel, b=32),
        out_shape=(square, square, square),
        scratch_shapes=[
            pltpu.VMEM((n, 2 * n), jnp.float32),
            pltpu.VMEM((n, 2 * n), jnp.float32),
            pltpu.VMEM((128, 2 * n), jnp.float32),
        ],
        name="factor",
    )(pieces)


def exchange(value, axis):
    return lax.all_to_all(value, axis, 0, 0, tiled=True)


def copied(value, axis):
    copies = jnp.broadcast_to(value, (lax.axis_size(axis), *value.shape))
    return exchange(copies, axis)


def row_major(value):
    return with_layout_constraint(value, Layout(major_to_minor=tuple(range(value.ndim))))


def transposed(value):
    rows = lax.axis_size("row")
    cols = lax.axis_size(COL)
    pairs = [(r * cols + c, c * rows + r) for r in range(rows) for c in range(cols)]
    return lax.ppermute(row_major(value), ("row", *COL), pairs)


def swapped(value):
    return lax.ppermute(value, COL[1], [(0, 1), (1, 0)])


def core_sum(value):
    return value + swapped(value)


def both_cores(lines):
    other = swapped(lines)
    second = lax.axis_index(COL[1]) == 1
    pair = [jnp.where(second, other, lines), jnp.where(second, lines, other)]
    return jnp.stack(pair, axis=1)


def join(parts):
    parts = parts.reshape(-1, *parts.shape[-3:])
    first, last = parts[:, 0], parts[:, 1]
    local = parts.shape[-1]
    return first.reshape(-1, local), last.reshape(-1, local)


def shards(matrix):
    row_blocks, width, _, _ = matrix.shape
    devices = lax.axis_size("row")
    row_index = lax.axis_index("row")
    col_index = lax.axis_index(COL)
    local = row_blocks * width
    part = width // devices
    dense = matrix.reshape(local, local)
    offsets = jnp.arange(local, dtype=jnp.int32)
    global_rows = (offsets // width * devices + row_index) * width + offsets % width
    global_cols = (offsets // width * devices + col_index) * width + offsets % width
    own = row_index * part
    corners = []
    sent = exchange(dense[:width].reshape(devices, part, local), "row")
    for panel in range(PANELS):
        start = (panel + 1) * width
        last = panel + 1 == PANELS
        below_cols = global_cols[None, :] >= start
        if panel == 0:
            x_own, c_own, *later = [
                jnp.where(below_cols, sent[source], 0.0) for source in range(PANELS + 1)
            ]
            x_rows = both_cores(copied(transposed(x_own), COL[0])).reshape(width, local)
        u_part = product(x_rows, dense)
        x_piece = lax.dynamic_slice_in_dim(x_rows, col_index * part, part, 0)
        gram_part = product(x_piece, x_rows, NT, highest)
        top_part = jnp.where(row_index == panel + 1, x_piece[:, :width], 0.0)
        first = jnp.concatenate([gram_part, top_part])
        rest = [c_own.reshape(2 * part, width)]
        if panel == 0:
            rest.append(x_own.reshape(2 * part, width))
        rest = jnp.concatenate(rest)
        each = u_part.reshape(devices, 2 * part, width)

        def spread_out(lines):
            return jnp.broadcast_to(lines, (devices, *lines.shape))

        if last:
            sums = jnp.sum(exchange(spread_out(first), "row"), axis=0)
        else:
            lines = spread_out(jnp.concatenate([first, rest]))
            merged = exchange(jnp.concatenate([lines, each], axis=1), "row")
            sums = jnp.sum(merged[:, : 2 * part], axis=0)
            merged = merged[:, 2 * part :]
        pieces = copied(sums, COL)
        if last:
            merged = exchange(jnp.concatenate([spread_out(rest), each], axis=1), "row")
            factors = factor(pieces)
            merged, (upper, lower, core) = lax.optimization_barrier((merged, factors))
        u_own = jnp.sum(merged[:, -2 * part :], axis=0).reshape(part, local)
        u_own = jnp.where(below_cols, u_own, 0.0)
        if not last:
            pair = transposed(jnp.stack([u_own, c_own]))
            pair = copied(pair, COL[0])
            factors = factor(pieces)
            pair, (upper, lower, core) = lax.optimization_barrier((pair, factors))
            u_rows, c_rows = join(both_cores(pair))
        c_cols = merged[:, : 2 * part].reshape(width, local)
        if panel == 0:
            x_cols = merged[:, 2 * part : 4 * part].reshape(width, local)

        def with_top(x, index):
            head = jnp.where(index == panel + 1, lower, 0.0)
            return jnp.concatenate([x[:, :width] + head, x[:, width:]], axis=1)

        v_cols = with_top(x_cols, col_index)
        v_rows = with_top(x_rows, row_index)
        w_own = u_own + product(lax.dynamic_slice_in_dim(lower, own, part, 0), c_cols)
        parts = [product(w_own, v_cols, NT)]
        if last:
            turned = transposed(w_own)
            own_sum = core_sum(row_major(parts[0])).reshape(part // 2, local)
            lines = copied(jnp.concatenate([turned, own_sum]), COL[0])
            sums = jnp.sum(lines[:, part:], axis=0).reshape(part, width)
            w_rows = both_cores(lines[:, :part]).reshape(width, local)
        else:
            w_rows = u_rows + product(lower, c_rows)
            across = lax.dynamic_slice_in_dim(x_cols[:, :width].T, own, part, 0)
            parts += [
                jnp.where(col_index == panel + 1, w_own[:, :width], 0.0),
                jnp.where(col_index == panel + 2, w_own[:, :width], 0.0),
                jnp.where(col_index == panel + 2, across, 0.0),
            ]
            sums = core_sum(row_major(jnp.concatenate(parts)))
            sums = jnp.sum(copied(sums, COL[0]), axis=0)
        shared = jnp.concatenate([w_own.reshape(2 * part, width), sums[: 3 * part]])
        shared = copied(shared, "row")
        w_cols = shared[:, : 2 * part].reshape(width, local)
        inner = shared[:, 2 * part : 3 * part].reshape(width, width)
        middle = 0.5 * product(product(core, inner), core, NT)
        y_cols = product(core, w_cols) - product(middle, v_cols)
        y_rows = product(core, w_rows) - product(middle, v_rows)
        dense = dense - product(
            jnp.concatenate([y_rows, v_rows]), jnp.concatenate([v_cols, y_cols]), TN
        )
        corners.append(upper)
        if last:
            break

        def y_of(w_t, v):
            return product(w_t, core, ((0,), (1,))) - product(v, middle, NT)

        def reduced(old, y, v, v_others, y_others):
            both = jnp.concatenate([y, v], axis=1)
            return old - product(both, jnp.concatenate([v_others, y_others]))

        w_top = shared[:, 3 * part : 4 * part].reshape(width, width)
        w_next = shared[:, 4 * part :].reshape(width, width)
        v_top = pieces[:, part:].reshape(width, width).T + upper
        y_top = y_of(w_top, v_top)
        v_next = sums[3 * part :]
        y_next = lax.dynamic_slice_in_dim(product(w_next, core, ((0,), (1,))), own, part, 0)
        y_next = y_next - product(v_next, middle, NT)
        x_cols = reduced(c_cols, y_top, v_top, v_cols, y_cols)
        x_rows = reduced(c_rows, y_top, v_top, v_rows, y_rows)
        c_own = reduced(later[0], y_next, v_next, v_cols, y_cols)
        x_cols = jnp.where(global_cols[None, :] >= start + width, x_cols, 0.0)
        x_rows = jnp.where(global_rows[None, :] >= start + width, x_rows, 0.0)
        c_own = jnp.where(global_cols[None, :] >= start + width, c_own, 0.0)
    slot_rows = offsets[:, None] < width
    slot_cols = offsets[None, :] < width
    for panel, upper in enumerate(corners):
        start = (panel + 1) * width
        pad = ((0, local - width), (0, local - width))
        at_cols = (col_index == panel) & slot_cols & (global_rows[:, None] >= start)
        new_cols = jnp.where(row_index == panel + 1, -jnp.pad(upper, pad), 0.0)
        dense = jnp.where(at_cols, new_cols, dense)
        at_rows = (row_index == panel) & slot_rows & (global_cols[None, :] >= start)
        new_rows = jnp.where(col_index == panel + 1, -jnp.pad(upper.T, pad), 0.0)
        dense = jnp.where(at_rows, new_rows, dense)
    return dense.reshape(matrix.shape)


def solution(mesh):
    split = Mesh(mesh.devices.reshape(mesh.shape["row"], 8, 2), ("row", "col_0", "col_1"))
    placed = (P(None, "row", None, COL),)
    return jax.shard_map(
        shards, mesh=split, in_specs=placed, out_specs=P(None, "row", None, COL), check_vma=False
    )
```

```python
import functools

import jax
import jax.numpy as jnp
from jax import lax
from jax.experimental import pallas as pl
from jax.experimental.layout import Layout, with_layout_constraint
from jax.experimental.pallas import tpu as pltpu
from jax.sharding import Mesh
from jax.sharding import PartitionSpec as P

PANELS = 2
COL = ("col_0", "col_1")

highest = lax.Precision.HIGHEST
high = lax.Precision.HIGH


def product(left, right, dims=((1,), (0,)), precision=high):
    return lax.dot_general(
        left, right, (dims, ((), ())), precision=precision, preferred_element_type=jnp.float32
    )


NT = ((1,), (1,))
TN = ((0,), (0,))
GROUP = 8


def row_of(tile, s):
    return jnp.broadcast_to(tile[s : s + 1, :], (8, 128))


class Elimination:
    def __init__(self, window, off, b):
        self.b, self.off, self.count = b, off, b // 8
        self.sublane = lax.broadcasted_iota(jnp.int32, (8, 128), 0)
        lanes = lax.broadcasted_iota(jnp.int32, (8, 128), 1)
        self.a = [window[8 * i : 8 * i + 8, :] for i in range(self.count)]
        self.e = [(lanes == self.sublane + 8 * i).astype(jnp.float32) for i in range(self.count)]
        zero = jnp.zeros((8, 128), jnp.float32)
        self.low = [zero] * self.count
        self.inv = [zero] * self.count

    def group(self, t):
        tiles = range(self.count)
        first = self.off + GROUP * t
        cols = [
            [jnp.broadcast_to(self.a[i][:, first + q : first + q + 1], (8, 128)) for i in tiles]
            for q in range(GROUP)
        ]
        for q in range(GROUP):
            inv = 1.0 / row_of(cols[q][t], q)
            here = self.sublane == q
            scale = [cols[q][i] * inv for i in tiles]
            scale[t] = jnp.where(here, 0.0, scale[t])
            for p in range(q + 1, GROUP):
                head = row_of(cols[p][t], q)
                for i in tiles:
                    cols[p][i] = cols[p][i] - scale[i] * head
            self.inv[t] = jnp.where(here, inv, self.inv[t])
            self.low[t] = jnp.where(here, self.e[t], self.low[t])
            row_a = row_of(self.a[t], q)
            row_e = row_of(self.e[t], q)
            for i in tiles:
                self.a[i] = self.a[i] - scale[i] * row_a
                self.e[i] = self.e[i] - scale[i] * row_e

    def inverse(self):
        inv = jnp.concatenate(self.inv, axis=0)
        return (jnp.concatenate(self.e, axis=0) * inv)[:, : self.b]

    def lower_inverse(self):
        inv = jnp.concatenate(self.inv, axis=0)
        return (jnp.concatenate(self.low, axis=0) * jnp.sqrt(inv))[:, : self.b]


def factor_kernel(pieces_ref, r_ref, l_ref, t_ref, aa, xb, wb, *, b):
    exact = functools.partial(product, precision=highest)
    n = r_ref.shape[0]
    part = pieces_ref.shape[1] // 2
    count = n // b
    rows = lax.broadcasted_iota(jnp.int32, (n, n), 0)
    cols = lax.broadcasted_iota(jnp.int32, (n, n), 1)
    for i in range(n // part):
        aa[part * i : part * i + part, :n] = pieces_ref[i, :part, :]
        xb[part * i : part * i + part, n:] = pieces_ref[i, part:, :]
    aa[:, n:] = (rows == cols).astype(jnp.float32)
    xb[:, :n] = xb[:, n:].T
    xb[:, n:] = jnp.zeros((n, n), jnp.float32)
    wb[...] = jnp.zeros((128, 2 * n), jnp.float32)
    lane = lax.broadcasted_iota(jnp.int32, (n, 128), 1)
    row = lax.broadcasted_iota(jnp.int32, (n, 128), 0)
    second = None
    for k in range(count + 1):
        lo, hi = k * b, (k + 1) * b
        win, off = lo // 128 * 128, lo % 128
        running = []
        if k < count:
            first = Elimination(aa[lo:hi, win : win + 128], off, b)
            running.append(first)
        if k > 0:
            second = Elimination(pivot, (lo - b) % 128, b)
            running.append(second)
        for t in range(b // 8):
            for one in running:
                one.group(t)
        if k < count:
            block = aa[lo:hi, :]
            if hi < n:
                wb[off : off + b, :] = exact(first.inverse(), block)
                keep = (lane[: n - hi] >= off) & (lane[: n - hi] < off + b)
                left = jnp.where(keep, aa[hi:, win : win + 128], 0.0)
                aa[hi:, :] = aa[hi:, :] - exact(left, wb[...])
            upper = exact(first.lower_inverse(), block)
            wide_row = lax.broadcasted_iota(jnp.int32, (b, 2 * n), 0) + lo
            wide_col = lax.broadcasted_iota(jnp.int32, (b, 2 * n), 1)
            upper = jnp.where(wide_col >= wide_row, upper, 0.0)
            upper = jnp.where(wide_col - n > wide_row, 0.0, upper)
            r_ref[lo:hi, :] = upper[:, :n]
        if k > 0:
            plo, phi = lo - b, lo
            pwin, poff = plo // 128 * 128, plo % 128
            xb[plo:phi, :] = exact(second.inverse(), pivot_row)
            keep = (lane >= poff) & (lane < poff + b) & ((row < plo) | (row >= phi))
            left = jnp.where(keep, xb[:, pwin : pwin + 128], 0.0)
            xb[...] = xb[...] - exact(left, xb[pwin : pwin + 128, :])
        if k < count:
            pivot_row = xb[lo:hi, :] + upper
            pivot = pivot_row[:, win : win + 128]
    l_ref[...] = r_ref[...].T
    t_ref[...] = xb[:, n:]


def factor(pieces):
    n = pieces.shape[-1]
    square = jax.ShapeDtypeStruct((n, n), jnp.float32)
    return pl.pallas_call(
        functools.partial(factor_kernel, b=32),
        out_shape=(square, square, square),
        scratch_shapes=[
            pltpu.VMEM((n, 2 * n), jnp.float32),
            pltpu.VMEM((n, 2 * n), jnp.float32),
            pltpu.VMEM((128, 2 * n), jnp.float32),
        ],
        name="factor",
    )(pieces)


def exchange(value, axis):
    return lax.all_to_all(value, axis, 0, 0, tiled=True)


def copied(value, axis):
    copies = jnp.broadcast_to(value, (lax.axis_size(axis), *value.shape))
    return exchange(copies, axis)


def row_major(value):
    return with_layout_constraint(value, Layout(major_to_minor=tuple(range(value.ndim))))


def transposed(value):
    rows = lax.axis_size("row")
    cols = lax.axis_size(COL)
    pairs = [(r * cols + c, c * rows + r) for r in range(rows) for c in range(cols)]
    return lax.ppermute(row_major(value), ("row", *COL), pairs)


def swapped(value):
    return lax.ppermute(value, COL[1], [(0, 1), (1, 0)])


def core_sum(value):
    return value + swapped(value)


def both_cores(lines):
    other = swapped(lines)
    second = lax.axis_index(COL[1]) == 1
    pair = [jnp.where(second, other, lines), jnp.where(second, lines, other)]
    return jnp.stack(pair, axis=1)


def join(parts):
    parts = parts.reshape(-1, *parts.shape[-3:])
    first, last = parts[:, 0], parts[:, 1]
    local = parts.shape[-1]
    return first.reshape(-1, local), last.reshape(-1, local)


def shards(matrix):
    row_blocks, width, _, _ = matrix.shape
    devices = lax.axis_size("row")
    row_index = lax.axis_index("row")
    col_index = lax.axis_index(COL)
    local = row_blocks * width
    part = width // devices
    dense = matrix.reshape(local, local)
    offsets = jnp.arange(local, dtype=jnp.int32)
    global_rows = (offsets // width * devices + row_index) * width + offsets % width
    global_cols = (offsets // width * devices + col_index) * width + offsets % width
    own = row_index * part
    corners = []
    sent = exchange(dense[:width].reshape(devices, part, local), "row")
    for panel in range(PANELS):
        start = (panel + 1) * width
        last = panel + 1 == PANELS
        below_cols = global_cols[None, :] >= start
        if panel == 0:
            x_own, c_own, *later = [
                jnp.where(below_cols, sent[source], 0.0) for source in range(PANELS + 1)
            ]
            x_rows = both_cores(copied(transposed(x_own), COL[0])).reshape(width, local)
        u_part = product(x_rows, dense)
        x_piece = lax.dynamic_slice_in_dim(x_rows, col_index * part, part, 0)
        gram_part = product(x_piece, x_rows, NT, highest)
        top_part = jnp.where(row_index == panel + 1, x_piece[:, :width], 0.0)
        first = jnp.concatenate([gram_part, top_part])
        rest = [c_own.reshape(2 * part, width)]
        if panel == 0:
            rest.append(x_own.reshape(2 * part, width))
        rest = jnp.concatenate(rest)
        each = u_part.reshape(devices, 2 * part, width)

        def spread_out(lines):
            return jnp.broadcast_to(lines, (devices, *lines.shape))

        if last:
            sums = jnp.sum(exchange(spread_out(first), "row"), axis=0)
        else:
            lines = spread_out(jnp.concatenate([first, rest]))
            merged = exchange(jnp.concatenate([lines, each], axis=1), "row")
            sums = jnp.sum(merged[:, : 2 * part], axis=0)
            c_cols = merged[:, 2 * part : 4 * part].reshape(width, local)
        pieces = copied(sums, COL)
        if last:
            merged = exchange(jnp.concatenate([spread_out(rest), each], axis=1), "row")
            factors = factor(pieces)
            merged, (upper, lower, core) = lax.optimization_barrier((merged, factors))
        u_own = jnp.sum(merged[:, -2 * part :], axis=0).reshape(part, local)
        u_own = jnp.where(below_cols, u_own, 0.0)
        if not last:
            pair = transposed(jnp.stack([u_own, c_own]))
            pair = copied(pair, COL[0])
            factors = factor(pieces)
            pair, (upper, lower, core) = lax.optimization_barrier((pair, factors))
            u_rows, c_rows = join(both_cores(pair))
        if last:
            c_cols = merged[:, : 2 * part].reshape(width, local)
        if panel == 0:
            x_cols = merged[:, 4 * part : 6 * part].reshape(width, local)

        def with_top(x, index):
            head = jnp.where(index == panel + 1, lower, 0.0)
            return jnp.concatenate([x[:, :width] + head, x[:, width:]], axis=1)

        v_cols = row_major(with_top(x_cols, col_index))
        v_rows = row_major(with_top(x_rows, row_index))
        w_own = u_own + product(lax.dynamic_slice_in_dim(lower, own, part, 0), c_cols)
        parts = [product(w_own, v_cols, NT)]
        if last:
            turned = transposed(w_own)
            own_sum = core_sum(row_major(parts[0])).reshape(part // 2, local)
            lines = copied(jnp.concatenate([turned, own_sum]), COL[0])
            sums = jnp.sum(lines[:, part:], axis=0).reshape(part, width)
            w_rows = both_cores(lines[:, :part]).reshape(width, local)
        else:
            w_rows = u_rows + product(lower, c_rows)
            across = lax.dynamic_slice_in_dim(x_cols[:, :width].T, own, part, 0)
            parts += [
                jnp.where(col_index == panel + 1, w_own[:, :width], 0.0),
                jnp.where(col_index == panel + 2, w_own[:, :width], 0.0),
                jnp.where(col_index == panel + 2, across, 0.0),
            ]
            sums = core_sum(row_major(jnp.concatenate(parts)))
            sums = jnp.sum(copied(sums, COL[0]), axis=0)
        shared = jnp.concatenate([w_own.reshape(2 * part, width), sums[: 3 * part]])
        shared = copied(shared, "row")
        w_cols = shared[:, : 2 * part].reshape(width, local)
        inner = shared[:, 2 * part : 3 * part].reshape(width, width)
        middle = 0.5 * product(product(core, inner), core, NT)
        y_cols = product(core, w_cols) - product(middle, v_cols)
        y_rows = product(core, w_rows) - product(middle, v_rows)
        y_cols, y_rows = row_major(y_cols), row_major(y_rows)
        dense = dense - product(
            jnp.concatenate([y_rows, v_rows]), jnp.concatenate([v_cols, y_cols]), TN
        )
        corners.append(upper)
        if last:
            break

        def y_of(w_t, v):
            return product(w_t, core, ((0,), (1,))) - product(v, middle, NT)

        def reduced(old, y, v, v_others, y_others):
            both = jnp.concatenate([y, v], axis=1)
            return old - product(both, jnp.concatenate([v_others, y_others]))

        w_top = shared[:, 3 * part : 4 * part].reshape(width, width)
        w_next = shared[:, 4 * part :].reshape(width, width)
        v_top = pieces[:, part:].reshape(width, width).T + upper
        y_top = y_of(w_top, v_top)
        v_next = sums[3 * part :]
        y_next = lax.dynamic_slice_in_dim(product(w_next, core, ((0,), (1,))), own, part, 0)
        y_next = y_next - product(v_next, middle, NT)
        x_cols = reduced(c_cols, y_top, v_top, v_cols, y_cols)
        x_rows = reduced(c_rows, y_top, v_top, v_rows, y_rows)
        c_own = reduced(later[0], y_next, v_next, v_cols, y_cols)
        x_cols = jnp.where(global_cols[None, :] >= start + width, x_cols, 0.0)
        x_rows = jnp.where(global_rows[None, :] >= start + width, x_rows, 0.0)
        c_own = jnp.where(global_cols[None, :] >= start + width, c_own, 0.0)
    slot_rows = offsets[:, None] < width
    slot_cols = offsets[None, :] < width
    for panel, upper in enumerate(corners):
        start = (panel + 1) * width
        pad = ((0, local - width), (0, local - width))
        at_cols = (col_index == panel) & slot_cols & (global_rows[:, None] >= start)
        new_cols = jnp.where(row_index == panel + 1, -jnp.pad(upper, pad), 0.0)
        dense = jnp.where(at_cols, new_cols, dense)
        at_rows = (row_index == panel) & slot_rows & (global_cols[None, :] >= start)
        new_rows = jnp.where(col_index == panel + 1, -jnp.pad(upper.T, pad), 0.0)
        dense = jnp.where(at_rows, new_rows, dense)
    return dense.reshape(matrix.shape)


def solution(mesh):
    split = Mesh(mesh.devices.reshape(mesh.shape["row"], 8, 2), ("row", "col_0", "col_1"))
    placed = (P(None, "row", None, COL),)
    return jax.shard_map(
        shards, mesh=split, in_specs=placed, out_specs=P(None, "row", None, COL), check_vma=False
    )
```
